512 devices in a mesh: pos: 16 (over y, z_hi), ky: 4 (over z_lo), kz: 8 (over x, core).
Axes of the slice: x: 4, y: 4, z: 16 (z_hi: 4, z_lo: 4; z = z_hi * 4 + z_lo), core: 2. Of those that a mesh axis runs over, the one named last changes fastest.
Arguments:
- cotangent: float32 [64, 64, 128, 64], P('pos', 'ky', 'kz'), may hold values from -6 to 6
- start_state: float32 [64, 64, 128, 64], P('pos', 'ky', 'kz'), may hold values from 0.1 to 2
- section_state: float32 [64, 64, 128, 64], P('pos', 'ky', 'kz'), may hold values from 0.1 to 2
- face_codes: int32 [64, 64, 128, 64], P('pos', 'ky', 'kz'), may hold values from 0 to 1295
- field_strength: float32 [3, 64], P(None, 'pos'), may hold values from -4 to 4
- velocity: float32 [64, 128, 64], P('ky', 'kz'), may hold values from -4 to 4
- shell_index: int32 [64, 128, 64], P('ky', 'kz'), may hold values from 0 to 63
- shell_out: float32 [64, 128, 64], P('ky', 'kz'), may hold values from 0.5 to 2
- shell_in: float32 [64, 128, 64], P('ky', 'kz'), may hold values from 0.0055242716 to 0.022097087
Outputs:
- state_adjoint: float32 [64, 64, 128, 64], P('pos', 'ky', 'kz')
- field_grad: float32 [3, 64], P(None, 'pos')
The draws below stay inside these ranges and needn't reach their ends.
Inputs may be any that keep to these rules, and one draw needn't show every extreme that they name: `face_codes`: each entry packs four digits of 0 to 5, one each for position, ky, kz, kx; the digit of dimension d is the entry divided by 6**d, modulo 6; digit // 3 is the upwind side and digit % 3 the reconstruction.
All inputs are finite; a program needn't handle non-finite values.
Results may differ from the reference program's by a relative error of at most 0.00011.
Values sent between devices are 32-bit elements; how exact they have to be, the bound alone decides.
No kernel may reach another device: no remote copies, remote signals or barrier semaphores. Data moves between devices by JAX's collectives and lax.ppermute only.
A program may use at most 64 MiB of HBM per device.

```python
import math
import jax
import jax.numpy as jnp
from jax import lax

KX = 64
KY = 64
KZ = 128
SHELLS = 64
POS = 64


def touch_ends(values, stream_key, least, top_value):
    dims = values.shape
    spot = [jax.random.randint(jax.random.fold_in(stream_key, axis), (), 0, dims[axis]) for axis in range(len(dims))]
    values = values.at[tuple(spot)].set(least)
    longest = dims.index(max(dims))
    spot[longest] = (spot[longest] + 1) % dims[longest]
    return values.at[tuple(spot)].set(top_value)


def block_scale(rng, extent, cuts, least, largest):
    gain, own = 1.0, jax.random.fold_in(rng, 6)
    for position, parts in cuts:
        steps = jnp.exp(jax.random.uniform(jax.random.fold_in(own, position), (parts,), jnp.float32, least / len(cuts), largest / len(cuts)))
        gain = gain * jnp.repeat(steps, extent[position] // parts).reshape([-1 if axis == position else 1 for axis in range(len(extent))])
    return gain


def bell_draw(rng, extent, deviation, limit, split=(), dtype=jnp.bfloat16):
    drawn = deviation * jax.random.normal(rng, extent, jnp.float32)
    if split:
        drawn = drawn * block_scale(rng, extent, split, -0.22, 0.18)
    return jnp.clip(drawn, -limit, limit).astype(dtype)


def setup_inputs(seed: int = 0) -> dict:
    key_list = jax.random.split(jax.random.key(seed), 10)
    return {
        "cotangent": bell_draw(key_list[0], (POS, KY, KZ, KX), 1.0, 6.0, ((0, 16), (1, 4), (2, 8)), jnp.float32),
        "start_state": jnp.clip(0.1 + 1.9 * jax.random.uniform(key_list[1], (POS, KY, KZ, KX), jnp.float32) ** block_scale(key_list[1], (POS, KY, KZ, KX), ((0, 16), (1, 4), (2, 8)), -0.2, 0.2), 0.1, 2.0),
        "section_state": jnp.clip(0.1 + 1.9 * jax.random.uniform(key_list[2], (POS, KY, KZ, KX), jnp.float32) ** block_scale(key_list[2], (POS, KY, KZ, KX), ((0, 16), (1, 4), (2, 8)), -0.2, 0.2), 0.1, 2.0),
        "face_codes": touch_ends(jax.random.randint(key_list[3], (POS, KY, KZ, KX), 0, 1296), jax.random.fold_in(key_list[3], 1), 0, 1295).astype(jnp.int32),
        "field_strength": bell_draw(key_list[4], (3, POS), 1.0, 4.0, ((1, 16),), jnp.float32),
        "velocity": bell_draw(key_list[5], (KY, KZ, KX), 1.0, 4.0, ((0, 4), (1, 8)), jnp.float32),
        "shell_index": touch_ends(jax.random.randint(key_list[6], (KY, KZ, KX), 0, SHELLS), jax.random.fold_in(key_list[6], 1), 0, SHELLS - 1).astype(jnp.int32),
        "shell_out": jnp.clip(jnp.exp(math.log(2.0) - 1.3862944 * jax.random.uniform(key_list[7], (KY, KZ, KX), jnp.float32) ** block_scale(key_list[7], (KY, KZ, KX), ((0, 4), (1, 8)), -0.2, 0.2)), 0.5, 2.0),
        "shell_in": jnp.clip(jnp.exp(math.log(0.022097087) - 1.3862944 * jax.random.uniform(key_list[8], (KY, KZ, KX), jnp.float32) ** block_scale(key_list[8], (KY, KZ, KX), ((0, 4), (1, 8)), -0.2, 0.2)), 0.0055242716, 0.022097087),
    }


time_step = 0.25
RECONSTRUCTION = ((0.0, -0.5, 0.0, 0.0, 0.0, 0.0), (1.0, 1.5, 0.5, 0.0, 0.0, 0.5), (0.0, 0.0, 0.5, 1.0, 1.5, 0.5), (0.0, 0.0, 0.0, 0.0, -0.5, 0.0))


def lookup(digits, values_table):
    summed = jnp.zeros(digits.shape, jnp.float32)
    for symbol in range(6):
        if values_table[symbol] != 0.0:
            summed = summed + jnp.where(digits == symbol, jnp.float32(values_table[symbol]), jnp.float32(0.0))
    return summed


def coefficients(face_codes, digit_place):
    digits = (face_codes // (6 ** digit_place)) % 6
    return [lookup(digits, weights_row) for weights_row in RECONSTRUCTION]


def neighbour(values, along_dim, offset, wrapped):
    if wrapped:
        return jnp.roll(values, -offset, along_dim)
    length = values.shape[along_dim]
    widths = [(0, 0)] * values.ndim
    widths[along_dim] = (2, 2)
    padded = jnp.pad(values, widths)
    return lax.slice_in_dim(padded, 2 + offset, 2 + offset + length, axis=along_dim)


def flux_adjoint(carried, face_codes, along_dim, wrapped):
    low_side, centre, high_side, far_side = coefficients(face_codes, along_dim)
    differ = carried - neighbour(carried, along_dim, 1, wrapped)
    return (neighbour(low_side * differ, along_dim, 1, wrapped) + centre * differ
            + neighbour(high_side * differ, along_dim, -1, wrapped)
            + neighbour(far_side * differ, along_dim, -2, wrapped))


def operator_adjoint(adjoint, field_strength, face_codes, velocity, shell_index, shell_out, shell_in):
    across = flux_adjoint(velocity[None] * adjoint, face_codes, 0, False)
    along_ky = flux_adjoint(adjoint, face_codes, 1, True)
    along_kz = flux_adjoint(adjoint, face_codes, 2, True)
    along_kx = flux_adjoint(adjoint, face_codes, 3, True)
    momentum = (along_kx, along_ky, along_kz)
    positions = adjoint.shape[0]
    weighted = (adjoint * shell_out[None]).reshape(positions, -1)
    indices = shell_index.reshape(-1).astype(jnp.int32)
    totals = jax.ops.segment_sum(weighted.T, indices, num_segments=SHELLS)
    returned = totals[indices].T.reshape(adjoint.shape) * shell_in[None]
    result = returned - across - adjoint
    for component in range(3):
        result = result - field_strength[component][:, None, None, None] * momentum[component]
    return result, momentum


def reference(cotangent, start_state, section_state, face_codes, field_strength, velocity, shell_index, shell_out, shell_in):
    normalizer = 1.0 / (KX * KY * KZ) ** 0.5
    applied, momentum = operator_adjoint(cotangent, field_strength, face_codes, velocity, shell_index, shell_out, shell_in)
    section_adjoint = 0.5 * cotangent + 0.5 * time_step * applied
    gradient = [-0.5 * time_step * jnp.sum(section_state * momentum[component], axis=(1, 2, 3)) for component in range(3)]
    applied, momentum = operator_adjoint(section_adjoint, field_strength, face_codes, velocity, shell_index, shell_out, shell_in)
    state_adjoint = 0.5 * cotangent + section_adjoint + time_step * applied
    gradient = [gradient[component] - time_step * jnp.sum(start_state * momentum[component], axis=(1, 2, 3)) for component in range(3)]
    field_grad = jnp.stack(gradient) * normalizer
    return state_adjoint, field_grad
```

```python
import jax
import jax.numpy as jnp
from jax import lax
from jax.sharding import PartitionSpec as P

KX = 64
KY = 64
KZ = 128
SHELLS = 64


time_step = 0.25
RECONSTRUCTION = (
    (0.0, -0.5, 0.0, 0.0, 0.0, 0.0),
    (1.0, 1.5, 0.5, 0.0, 0.0, 0.5),
    (0.0, 0.0, 0.5, 1.0, 1.5, 0.5),
    (0.0, 0.0, 0.0, 0.0, -0.5, 0.0),
)


def shifted_2(array, axis, by):
    count = lax.axis_size(axis)
    pairs = [(i, i + by) for i in range(count) if 0 <= i + by < count]
    return lax.ppermute(array, axis, pairs)


def from_behind(value, axis, steps):
    count = lax.axis_size(axis)
    pairs = [(source, (source + steps) % count) for source in range(count)]
    return lax.ppermute(value, axis, pairs)


def padded_2(array, sides, width, wrap):
    for axis, dim in sides:
        count, length = (lax.axis_size(axis), array.shape[dim])
        up = [(i, (i + 1) % count) for i in range(count if wrap else count - 1)]
        down = [(j, i) for i, j in up]
        last = lax.slice_in_dim(array, length - width, length, axis=dim)
        first = lax.slice_in_dim(array, 0, width, axis=dim)
        before = lax.ppermute(last, axis, up)
        after = lax.ppermute(first, axis, down)
        array = jnp.concatenate([before, array, after], axis=dim)
    return array


def sum_over_momentum(value):
    count = lax.axis_size("ky") * lax.axis_size("kz")
    copies = jnp.broadcast_to(value[None], (count,) + value.shape)
    return jnp.sum(lax.all_to_all(copies, ("ky", "kz"), 0, 0), axis=0)


def lookup(digits, values_table):
    summed = jnp.zeros(digits.shape, jnp.float32)
    for symbol in range(6):
        if values_table[symbol] != 0.0:
            summed = summed + jnp.where(
                digits == symbol, jnp.float32(values_table[symbol]), jnp.float32(0.0)
            )
    return summed


def coefficients(face_codes, digit_place):
    digits = face_codes // 6**digit_place % 6
    return [lookup(digits, weights_row) for weights_row in RECONSTRUCTION]


def differences(carried, following, along_dim):
    length = carried.shape[along_dim]
    shifted = jnp.concatenate(
        [lax.slice_in_dim(carried, 1, length, axis=along_dim), following], axis=along_dim
    )
    return carried - shifted


def rim_terms(differ, coeff_sets):
    low_side, centre, high_side, far_side = coeff_sets
    return jnp.stack([low_side * differ, high_side * differ, far_side * differ])


def finish(padded, differ, coeff_sets, along_dim, length):
    centre = coeff_sets[1]
    return (
        lax.slice_in_dim(padded[0], 3, 3 + length, axis=along_dim)
        + centre * differ
        + lax.slice_in_dim(padded[1], 1, 1 + length, axis=along_dim)
        + lax.slice_in_dim(padded[2], 0, length, axis=along_dim)
    )


def operator_adjoint(
    adjoint, field_strength, coeff_all, velocity, shell_table, shell_out, shell_in
):
    positions, rows_ky, rows_kz = (adjoint.shape[0], adjoint.shape[1], adjoint.shape[2])
    carried = velocity[None] * adjoint
    following = shifted_2(lax.slice_in_dim(carried, 0, 1, axis=0), "pos", -1)
    differ_pos = differences(carried, following, 0)
    next_ky = from_behind(lax.slice_in_dim(adjoint, 0, 1, axis=1), "ky", -1)
    next_kz = from_behind(lax.slice_in_dim(adjoint, 0, 1, axis=2), "kz", -1)
    differ_ky = differences(adjoint, next_ky, 1)
    differ_kz = differences(adjoint, next_kz, 2)
    padded_pos = padded_2(rim_terms(differ_pos, coeff_all[0]), (("pos", 1),), 2, False)
    across = finish(padded_pos, differ_pos, coeff_all[0], 0, positions)
    terms_ky = rim_terms(differ_ky, coeff_all[1])
    terms_kz = rim_terms(differ_kz, coeff_all[2])
    padded_ky = padded_2(terms_ky, (("ky", 2),), 2, True)
    padded_kz = padded_2(terms_kz, (("kz", 3),), 2, True)
    along_ky = finish(padded_ky, differ_ky, coeff_all[1], 1, rows_ky)
    along_kz = finish(padded_kz, differ_kz, coeff_all[2], 2, rows_kz)
    low_side, centre, high_side, far_side = coeff_all[3]
    differ_kx = adjoint - jnp.roll(adjoint, -1, 3)
    along_kx = (
        jnp.roll(low_side * differ_kx, -1, 3)
        + centre * differ_kx
        + jnp.roll(high_side * differ_kx, 1, 3)
        + jnp.roll(far_side * differ_kx, 2, 3)
    )
    momentum = (along_kx, along_ky, along_kz)
    weighted = (adjoint * shell_out[None]).reshape(positions, -1)
    local_totals = jnp.dot(
        weighted, shell_table, precision=lax.Precision.HIGHEST, preferred_element_type=jnp.float32
    )
    totals = sum_over_momentum(local_totals)
    returned = jnp.dot(
        totals, shell_table.T, precision=lax.Precision.HIGHEST, preferred_element_type=jnp.float32
    )
    returned = returned.reshape(adjoint.shape) * shell_in[None]
    result = returned - across - adjoint
    for component in range(3):
        result = result - field_strength[component][:, None, None, None] * momentum[component]
    return (result, momentum)


def shards(
    cotangent,
    start_state,
    section_state,
    face_codes,
    field_strength,
    velocity,
    shell_index,
    shell_out,
    shell_in,
):
    coeff_all = [coefficients(face_codes, digit_place) for digit_place in range(4)]
    indices = shell_index.reshape(-1)
    shell_table = (indices[:, None] == jnp.arange(SHELLS, dtype=jnp.int32)[None, :]).astype(
        jnp.float32
    )
    applied, momentum = operator_adjoint(
        cotangent, field_strength, coeff_all, velocity, shell_table, shell_out, shell_in
    )
    section_adjoint = 0.5 * cotangent + 0.5 * time_step * applied
    local_grad = jnp.stack(
        [
            -0.5 * time_step * jnp.sum(section_state * momentum[component], axis=(1, 2, 3))
            for component in range(3)
        ]
    )
    applied, momentum = operator_adjoint(
        section_adjoint, field_strength, coeff_all, velocity, shell_table, shell_out, shell_in
    )
    state_adjoint = 0.5 * cotangent + section_adjoint + time_step * applied
    local_grad = local_grad - jnp.stack(
        [
            time_step * jnp.sum(start_state * momentum[component], axis=(1, 2, 3))
            for component in range(3)
        ]
    )
    normalizer = 1.0 / (KX * KY * KZ) ** 0.5
    field_grad = sum_over_momentum(local_grad) * normalizer
    return (state_adjoint, field_grad)


def solution(mesh):
    return jax.shard_map(
        shards,
        mesh=mesh,
        in_specs=(
            P("pos", "ky", "kz", None),
            P("pos", "ky", "kz", None),
            P("pos", "ky", "kz", None),
            P("pos", "ky", "kz", None),
            P(None, "pos"),
            P("ky", "kz", None),
            P("ky", "kz", None),
            P("ky", "kz", None),
            P("ky", "kz", None),
        ),
        out_specs=(P("pos", "ky", "kz", None), P(None, "pos")),
        check_vma=False,
    )
```

```python
import functools

import jax
import jax.numpy as jnp
from jax import lax
from jax.experimental import pallas as pl
from jax.experimental.pallas import tpu as pltpu
from jax.sharding import PartitionSpec as P


KX = 64
KY = 64
KZ = 128
SHELLS = 64
X = 4
R = 8
Z = 16
L = 128
HALF = 64
time_step = 0.25
F32 = jnp.float32
BF16 = jnp.bfloat16
FULL = (X, R, Z, L)
VMEM_LIMIT = 24 * 1024 * 1024


def lanes(shape):
    return lax.broadcasted_iota(jnp.int32, shape, len(shape) - 1)


def pack(low, high):
    return jnp.concatenate([low, high], axis=-1)


def swap(row):
    return pltpu.roll(row, HALF, row.ndim - 1)


def split6(code):
    whole = jnp.floor((code + 0.5) * (1.0 / 6.0))
    return whole, code - 6.0 * whole


def digits_of(code):
    rest, pos = split6(code)
    rest, ky = split6(rest)
    kx, kz = split6(rest)
    return pos, ky, kz, kx


def c_low(digit):
    return jnp.where(digit == 1.0, -0.5, 0.0)


def c_far(digit):
    return jnp.where(digit == 4.0, -0.5, 0.0)


def c_high(digit):
    return jnp.where(digit == 5.0, 0.5, jnp.maximum(0.5 * digit - 0.5, 0.0))


def terms(digit, differ):
    half = -0.5 * differ
    low = jnp.where(digit == 1.0, half, 0.0)
    far = jnp.where(digit == 4.0, half, 0.0)
    high = c_high(digit) * differ
    return low, differ - low - high - far, high, far


def coeffs(digit):
    low, high, far = c_low(digit), c_high(digit), c_far(digit)
    return low, 1.0 - low - high - far, high, far


class Shifts:
    def __init__(self):
        lane = lanes((Z, L))
        self.low = lane < HALF
        kx = lane & (HALF - 1)
        self.kx_first, self.kx_second = kx == 0, kx < 2
        self.kx_last, self.kx_pair = kx == HALF - 1, kx >= HALF - 2
        z = lax.broadcasted_iota(jnp.int32, (Z, L), 0)
        self.z0, self.z1 = z == 0, z == 1
        self.z_last, self.z_before = z == Z - 1, z == Z - 2

    def kx(self, row, by):
        mask, wrapped = {
            -1: (self.kx_last, HALF - 1),
            -2: (self.kx_pair, HALF - 2),
            1: (self.kx_first, HALF + 1),
            2: (self.kx_second, HALF + 2),
        }[by]
        return jnp.where(mask, pltpu.roll(row, wrapped, 1), pltpu.roll(row, by % L, 1))

    def kz_next(self, row, after):
        return jnp.where(self.z_last, after, pltpu.roll(row, Z - 1, 0))

    def kz_next2(self, row, after, after2):
        return jnp.where(self.z_last, after2, jnp.where(self.z_before, after, pltpu.roll(row, Z - 2, 0)))

    def kz_prev(self, row, before):
        return jnp.where(self.z0, before, pltpu.roll(row, 1, 0))

    def kz_prev2(self, row, before, before2):
        return jnp.where(self.z0, before2, jnp.where(self.z1, before, pltpu.roll(row, 2, 0)))


def ky_up_rows(array):
    return array, swap(array)


def ky_down_rows(array):
    return swap(array), array


def along_kx(sh, u, digit):
    low, centre, high, far = terms(digit, u - sh.kx(u, -1))
    return sh.kx(low, -1) + centre + sh.kx(high, 1) + sh.kx(far, 2)


def along_kz(sh, u, digit, above, t_above, digit_b, below, s_below):
    low, centre, high, far = terms(digit, u - sh.kz_next(u, above))
    edge = below - u[0:1]
    return (
        sh.kz_next(low, t_above)
        + centre
        + sh.kz_prev(high, c_high(digit_b) * edge)
        + sh.kz_prev2(far, c_far(digit_b) * edge, s_below)
    )


def along_ky(sh, rows, digit_rows, above, t_above, digit_b, below, s_below):
    nxt = rows[1:] + [jnp.where(sh.low, swap(rows[0]), above)]
    parts = [terms(digit_rows[r], rows[r] - nxt[r]) for r in range(R)]
    edge = below - rows[0]
    low_after = jnp.where(sh.low, swap(parts[0][0]), t_above)
    high_before = jnp.where(sh.low, c_high(digit_b) * edge, swap(parts[R - 1][2]))
    far_before = jnp.where(sh.low, c_far(digit_b) * edge, swap(parts[R - 1][3]))
    far_before2 = jnp.where(sh.low, s_below, swap(parts[R - 2][3]))
    lows = [p[0] for p in parts] + [low_after]
    highs = [high_before] + [p[2] for p in parts]
    fars = [far_before2, far_before] + [p[3] for p in parts]
    return [lows[r + 1] + parts[r][1] + highs[r] + fars[r] for r in range(R)]


def gather(table, index):
    wide = jnp.broadcast_to(table, (Z, L))
    return jnp.take_along_axis(wide, index, axis=1)


def pos_terms(rows, digit_rows):
    nxt = rows[1:] + [None]
    parts = [
        terms(digit_rows[x], rows[x] - nxt[x] if nxt[x] is not None else rows[x])
        for x in range(X)
    ]
    out = []
    for x in range(X):
        value = parts[x][1]
        if x + 1 < X:
            value = value + parts[x + 1][0]
        if x >= 1:
            value = value + parts[x - 1][2]
        if x >= 2:
            value = value + parts[x - 2][3]
        out.append(value)
    return out


def pos_corrections(first, digit_last, digit_b, below, s_below, above, t_above):
    edge = below - first
    low, centre, _, _ = coeffs(digit_last)
    return (
        c_high(digit_b) * edge + s_below,
        c_far(digit_b) * edge,
        -low * above,
        t_above - centre * above,
    )


def shell_sums(w_ref, shell_ref):
    shells = lax.broadcasted_iota(jnp.int32, (SHELLS, L), 0)

    def body(r, total):
        left = jnp.concatenate(
            [w_ref[r, pl.ds(z, 2 * X, stride=Z), :] for z in range(Z)], axis=1
        ).astype(BF16)
        right = jnp.concatenate(
            [
                jnp.where(shells == shell_ref[r, z : z + 1, :], 1.0, 0.0).astype(BF16)
                for z in range(Z)
            ],
            axis=1,
        )
        return total + lax.dot_general(
            left, right, (((1,), (1,)), ((), ())), preferred_element_type=F32
        )

    both = lax.fori_loop(0, R, body, jnp.zeros((2 * X, SHELLS), F32))
    return both[:X] + both[X:]


def put_weighted(w_ref, r, x, value):
    head = value.astype(BF16).astype(F32)
    w_ref[r, x * Z : (x + 1) * Z, :] = head
    w_ref[r, (X + x) * Z : (X + x + 1) * Z, :] = value - head


def edges_kernel(u_ref, code_ref, start_ref, vel_ref, pos_up, pos_down, ky_up, ky_down, kz_up, kz_down):
    def whole(ref, x, r):
        return pack(ref[x, r], ref[x, r + R])

    def plane(ref, x, z):
        both = ref[x, :, z, :]
        return pack(both[:R], both[R:])

    for r in range(R):
        v = pack(vel_ref[r], vel_ref[r + R])
        u0, u1, u2, u3 = (v * whole(u_ref, x, r) for x in range(X))
        d0, d2, d3 = (split6(whole(code_ref, x, r).astype(F32))[1] for x in (0, 2, 3))
        pos_up[0, r] = d3
        pos_up[1, r] = u3
        pos_up[2, r] = c_far(d2) * (u2 - u3)
        pos_down[0, r] = u0
        pos_down[1, r] = c_low(d0) * (u0 - u1)
    for x in range(X):
        k = 2 * R - 1
        d_last = digits_of(code_ref[x, k].astype(F32))[1]
        d_prev = digits_of(code_ref[x, k - 1].astype(F32))[1]
        last, prev = u_ref[x, k], u_ref[x, k - 1]
        ky_up[0, x] = pack(d_last, last)
        ky_up[1, x] = pack(c_far(d_prev) * (prev - last), start_ref[x, k])
        ky_up[2, x] = pack(start_ref[x, k - 1], start_ref[x, k - 1])
        d_first = digits_of(code_ref[x, 0].astype(F32))[1]
        first, second = u_ref[x, 0], u_ref[x, 1]
        ky_down[0, x] = pack(first, c_low(d_first) * (first - second))
        ky_down[1, x] = pack(start_ref[x, 0], start_ref[x, 1])
        d_last = digits_of(plane(code_ref, x, Z - 1).astype(F32))[2]
        d_prev = digits_of(plane(code_ref, x, Z - 2).astype(F32))[2]
        last, prev = plane(u_ref, x, Z - 1), plane(u_ref, x, Z - 2)
        kz_up[0, x] = d_last
        kz_up[1, x] = last
        kz_up[2, x] = c_far(d_prev) * (prev - last)
        kz_up[3, x] = plane(start_ref, x, Z - 1)
        kz_up[4, x] = plane(start_ref, x, Z - 2)
        d_first = digits_of(plane(code_ref, x, 0).astype(F32))[2]
        first, second = plane(u_ref, x, 0), plane(u_ref, x, 1)
        kz_down[0, x] = first
        kz_down[1, x] = c_low(d_first) * (first - second)
        kz_down[2, x] = plane(start_ref, x, 0)
        kz_down[3, x] = plane(start_ref, x, 1)


def first_sums_kernel(u_ref, code_ref, vel_ref, shell_ref, out_ref, in_ref, u_p, code_p, fields_p, shell_p, sums, w_ref):
    for r in range(R):
        fields_p[0, r] = pack(vel_ref[r], vel_ref[r + R])
        weight = pack(out_ref[r], out_ref[r + R])
        fields_p[1, r] = weight
        fields_p[2, r] = pack(in_ref[r], in_ref[r + R])
        shell_p[r] = pack(shell_ref[r], shell_ref[r + R])
        for x in range(X):
            u = pack(u_ref[x, r], u_ref[x, r + R])
            u_p[x, r] = u
            code_p[x, r] = pack(code_ref[x, r], code_ref[x, r + R]).astype(F32)
            put_weighted(w_ref, r, x, weight * u)
    totals = shell_sums(w_ref, shell_p)
    tile = jnp.concatenate([totals, jnp.zeros_like(totals)], axis=1)
    for n in range(sums.shape[0]):
        sums[n] = tile


def add_copies(got):
    total = got[0]
    for n in range(1, got.shape[0]):
        total = total + got[n]
    return total


def momentum_terms(sh, field, x, u, digit, k_ky, kz_rows):
    ks = (along_kx(sh, u, digit[3]), k_ky, along_kz(sh, u, digit[2], *kz_rows))
    return ks, field[0, x] * ks[0] + field[1, x] * ks[1] + field[2, x] * ks[2]


def face(digit, f_prev, f, f_next, f_next2):
    low, centre, high, far = coeffs(digit)
    return low * f_prev + centre * f + high * f_next + far * f_next2


def section_kernel(
    field, u_p, code_p, fields_p, shell_p, section_ref, start_ref, got_sums,
    ky_up, ky_down, kz_up, kz_down,
    partial, slopes, grads,
):
    sh = Shifts()
    totals = add_copies(got_sums)

    def body(x, carry):
        rows = [u_p[x, r] for r in range(R)]
        digit = [digits_of(code_p[x, r]) for r in range(R)]
        start = [pack(start_ref[x, r], start_ref[x, r + R]) for r in range(R)]
        d_b, below = ky_up_rows(ky_up[0, x])
        s_below, f_below = ky_up_rows(ky_up[1, x])
        f_below2 = ky_up[2, x]
        above, t_above = ky_down_rows(ky_down[0, x])
        f_above, f_above2 = ky_down_rows(ky_down[1, x])
        k_ky = along_ky(sh, rows, [d[1] for d in digit], above, t_above, d_b, below, s_below)
        before = [jnp.where(sh.low, f_below, swap(start[R - 1]))] + start[:-1]
        after = start + [
            jnp.where(sh.low, swap(start[0]), f_above),
            jnp.where(sh.low, swap(start[1]), f_above2),
        ]
        faces = [face(digit[r][1], before[r], start[r], after[r + 1], after[r + 2]) for r in range(R)]
        face_b = face(d_b, f_below2, f_below, start[0], start[1])
        faces_before = [jnp.where(sh.low, face_b, swap(faces[R - 1]))] + faces[:-1]
        grad_x = [jnp.zeros((Z, L), F32)] * 3
        for r in range(R):
            u, f, d = rows[r], start[r], digit[r]
            up = [kz_up[n, x, r : r + 1, :] for n in range(5)]
            down = [kz_down[n, x, r : r + 1, :] for n in range(4)]
            ks, push = momentum_terms(sh, field, x, u, d, k_ky[r], (down[0], down[1], up[0], up[1], up[2]))
            sec = pack(section_ref[x, r], section_ref[x, r + R])
            grad_x = [g + sec * k for g, k in zip(grad_x, ks)]
            partial[x, r] = push
            faces_kx = face(d[3], sh.kx(f, 1), f, sh.kx(f, -1), sh.kx(f, -2))
            slopes[0, x, r] = faces_kx - sh.kx(faces_kx, 1)
            slopes[1, x, r] = faces[r] - faces_before[r]
            faces_kz = face(
                d[2], sh.kz_prev(f, up[3]), f, sh.kz_next(f, down[2]), sh.kz_next2(f, down[2], down[3])
            )
            slopes[2, x, r] = faces_kz - sh.kz_prev(faces_kz, face(up[0], up[4], up[3], f[0:1], f[1:2]))
        for c in range(3):
            grads[c, x] = grad_x[c]
        return carry

    lax.fori_loop(0, X, body, 0)

    def finish(r, carry):
        v, back, shell = fields_p[0, r], fields_p[2, r], shell_p[r]
        us = [u_p[x, r] for x in range(X)]
        k_pos = pos_terms([v * u for u in us], [split6(code_p[x, r])[1] for x in range(X)])
        for x in range(X):
            applied = back * gather(totals[x : x + 1], shell) - partial[x, r] - k_pos[x] - us[x]
            partial[x, r] = 0.5 * us[x] + (0.5 * time_step) * applied
        return carry

    lax.fori_loop(0, R, finish, 0)


def section_edges_kernel(partial, u_p, code_p, fields_p, got_up, got_down, section, pos_up, pos_down):
    def body(r, carry):
        v = fields_p[0, r]
        d0, d2, d3 = (split6(code_p[x, r])[1] for x in (0, 2, 3))
        more = pos_corrections(
            v * u_p[0, r], d3, got_up[0, r], got_up[1, r], got_up[2, r], got_down[0, r], got_down[1, r]
        )
        m = []
        for x in range(X):
            value = partial[x, r] - (0.5 * time_step) * more[x]
            section[x, r] = value
            m.append(v * value)
        pos_up[0, r] = m[3]
        pos_up[1, r] = c_far(d2) * (m[2] - m[3])
        pos_down[0, r] = m[0]
        pos_down[1, r] = c_low(d0) * (m[0] - m[1])
        return carry

    lax.fori_loop(0, R, body, 0)


def momentum_edges_kernel(section, code_p, ky_up, ky_down, kz_up, kz_down):
    low_half = lanes((Z, L)) < HALF
    for x in range(X):
        last, prev = section[x, R - 1], section[x, R - 2]
        far = c_far(digits_of(code_p[x, R - 2])[1]) * (prev - last)
        ky_up[x] = jnp.where(low_half, swap(last), far)
        first, second = section[x, 0], section[x, 1]
        low = c_low(digits_of(code_p[x, 0])[1]) * (first - second)
        ky_down[x] = jnp.where(low_half, first, swap(low))
        last, prev = section[x, :, Z - 1, :], section[x, :, Z - 2, :]
        kz_up[0, x] = last
        kz_up[1, x] = c_far(digits_of(code_p[x, :, Z - 2, :])[2]) * (prev - last)
        first, second = section[x, :, 0, :], section[x, :, 1, :]
        kz_down[0, x] = first
        kz_down[1, x] = c_low(digits_of(code_p[x, :, 0, :])[2]) * (first - second)


def second_sums_kernel(section, fields_p, shell_p, slopes, grads, sums, w_ref):
    row = lax.broadcasted_iota(jnp.int32, (X, SHELLS), 0)
    column = lax.broadcasted_iota(jnp.int32, (X, SHELLS), 1)
    inner = jnp.zeros((X, SHELLS), F32)
    for x in range(X):
        parts = [(0.5 * time_step) * grads[c, x] for c in range(3)]
        for r in range(R):
            value = section[x, r]
            put_weighted(w_ref, r, x, fields_p[1, r] * value)
            parts = [p + time_step * (value * slopes[c, x, r]) for c, p in enumerate(parts)]
        for c in range(3):
            whole = jnp.sum(jnp.sum(parts[c], axis=0, keepdims=True), axis=1, keepdims=True)
            inner = inner - jnp.where((row == x) & (column == c), whole, 0.0)
    tile = jnp.concatenate([shell_sums(w_ref, shell_p), inner], axis=1)
    for n in range(sums.shape[0]):
        sums[n] = tile


def interior_kernel(field, section, u_p, code_p, fields_p, first_up, first_kz, ky_up, ky_down, kz_up, kz_down, partial):
    sh = Shifts()

    def body(x, carry):
        rows = [section[x, r] for r in range(R)]
        digit = [digits_of(code_p[x, r]) for r in range(R)]
        below, s_below = ky_up_rows(ky_up[x])
        above, t_above = ky_down_rows(ky_down[x])
        k_ky = along_ky(sh, rows, [d[1] for d in digit], above, t_above, first_up[0, x], below, s_below)
        for r in range(R):
            here = slice(r, r + 1)
            kz_rows = (
                kz_down[0, x, here, :],
                kz_down[1, x, here, :],
                first_kz[0, x, here, :],
                kz_up[0, x, here, :],
                kz_up[1, x, here, :],
            )
            _, push = momentum_terms(sh, field, x, rows[r], digit[r], k_ky[r], kz_rows)
            partial[x, r] = push
        return carry

    lax.fori_loop(0, X, body, 0)

    def finish(r, carry):
        v = fields_p[0, r]
        ms = [section[x, r] for x in range(X)]
        k_pos = pos_terms([v * m for m in ms], [split6(code_p[x, r])[1] for x in range(X)])
        for x in range(X):
            partial[x, r] = (
                0.5 * u_p[x, r] + ms[x] - time_step * (partial[x, r] + k_pos[x] + ms[x])
            )
        return carry

    lax.fori_loop(0, R, finish, 0)


def result_kernel(
    scale, partial, section, code_p, fields_p, shell_p, first_up, got_up, got_down, got_sums, state, grad
):
    totals = add_copies(got_sums)
    for r in range(R):
        v, back, shell = fields_p[0, r], fields_p[2, r], shell_p[r]
        more = pos_corrections(
            v * section[0, r], split6(code_p[3, r])[1], first_up[0, r], got_up[0, r], got_up[1, r],
            got_down[0, r], got_down[1, r],
        )
        for x in range(X):
            value = partial[x, r] + time_step * (back * gather(totals[x : x + 1], shell) - more[x])
            state[x, r] = value[:, :HALF]
            state[x, r + R] = value[:, HALF:]
    row = lax.broadcasted_iota(jnp.int32, (X, L), 0)
    column = lanes((X, L))
    for c in range(3):
        spread = jnp.broadcast_to(totals[:, SHELLS + c : SHELLS + c + 1], (X, L))
        line = jnp.sum(jnp.where(row == column, spread, 0.0), axis=0, keepdims=True)
        grad[c : c + 1, :] = line[:, :X] * scale


def call(kernel, outs, args, scalars=0, scratch=(), ops=0):
    shapes = [jax.ShapeDtypeStruct(shape, F32 if dtype is None else dtype) for shape, dtype in outs]
    moved = sum(4 * a.size for a in args) + sum(4 * s.size for s in shapes)
    vmem = pl.BlockSpec(memory_space=pltpu.VMEM)
    smem = pl.BlockSpec(memory_space=pltpu.SMEM)
    return pl.pallas_call(
        kernel,
        out_shape=shapes,
        in_specs=[smem] * scalars + [vmem] * (len(args) - scalars),
        out_specs=[vmem] * len(shapes),
        scratch_shapes=list(scratch),
        compiler_params=pltpu.CompilerParams(vmem_limit_bytes=VMEM_LIMIT),
        cost_estimate=pl.CostEstimate(flops=ops, bytes_accessed=moved, transcendentals=0),
    )(*args)


def shift(array, axis, by, wrap=True):
    count = lax.axis_size(axis)
    pairs = [(i, (i + by) % count) for i in range(count) if wrap or 0 <= i + by < count]
    return lax.ppermute(array, axis, pairs)


def shift_both(up, down, axis, wrap=True):
    up = shift(up, axis, 1, wrap)
    down = shift(down, axis, -1, wrap)
    return up, down


def exchange(copies):
    return lax.all_to_all(copies, ("ky", "kz"), 0, 0)


def shards(
    cotangent,
    start_state,
    section_state,
    face_codes,
    field_strength,
    velocity,
    shell_index,
    shell_out,
    shell_in,
):
    members = lax.axis_size("ky") * lax.axis_size("kz")
    plane, ky_plane, kz_plane = (R, Z, L), (X, Z, L), (X, R, L)
    w_scratch = [pltpu.VMEM((R, 2 * X * Z, L), F32)]
    sums_shape = ((members, X, L), None)
    up, down, ky_up, ky_down, kz_up, kz_down = call(
        edges_kernel,
        [((3,) + plane, None), ((2,) + plane, None), ((3,) + ky_plane, None), ((2,) + ky_plane, None),
         ((5,) + kz_plane, None), ((4,) + kz_plane, None)],
        [cotangent, face_codes, start_state, velocity],
        ops=4_000_000,
    )
    cotangent, up, down, ky_up, ky_down, kz_up, kz_down = lax.optimization_barrier(
        (cotangent, up, down, ky_up, ky_down, kz_up, kz_down)
    )
    up, down = shift_both(up, down, "pos", False)
    ky_up, ky_down = shift_both(ky_up, ky_down, "ky")
    kz_up, kz_down = shift_both(kz_up, kz_down, "kz")
    u_p, code_p, fields_p, shell_p, sums = call(
        first_sums_kernel,
        [(FULL, None), (FULL, None), ((3,) + plane, None), (plane, jnp.int32), sums_shape],
        [cotangent, face_codes, velocity, shell_index, shell_out, shell_in],
        scratch=w_scratch,
        ops=8_000_000,
    )
    sums = exchange(sums)
    partial, slopes, grads = call(
        section_kernel,
        [(FULL, None), ((3,) + FULL, None), ((3, X, Z, L), None)],
        [field_strength, u_p, code_p, fields_p, shell_p, section_state, start_state, sums, ky_up, ky_down, kz_up, kz_down],
        scalars=1,
        ops=16_000_000,
    )
    section, up2, down2 = call(
        section_edges_kernel,
        [(FULL, None), ((2,) + plane, None), ((2,) + plane, None)],
        [partial, u_p, code_p, fields_p, up, down],
        ops=2_000_000,
    )
    up2, down2 = shift_both(up2, down2, "pos", False)
    ky_up2, ky_down2, kz_up2, kz_down2 = call(
        momentum_edges_kernel,
        [(ky_plane, None), (ky_plane, None), ((2,) + kz_plane, None), ((2,) + kz_plane, None)],
        [section, code_p],
        ops=1_000_000,
    )
    section, ky_up2, ky_down2, kz_up2, kz_down2 = lax.optimization_barrier(
        (section, ky_up2, ky_down2, kz_up2, kz_down2)
    )
    ky_up2, ky_down2 = shift_both(ky_up2, ky_down2, "ky")
    kz_up2, kz_down2 = shift_both(kz_up2, kz_down2, "kz")
    (sums2,) = call(
        second_sums_kernel, [sums_shape], [section, fields_p, shell_p, slopes, grads], scratch=w_scratch, ops=4_000_000
    )
    sums2 = exchange(sums2)
    (partial2,) = call(
        interior_kernel,
        [(FULL, None)],
        [field_strength, section, u_p, code_p, fields_p, ky_up, kz_up, ky_up2, ky_down2, kz_up2, kz_down2],
        scalars=1,
        ops=8_000_000,
    )
    state_adjoint, field_grad = call(
        functools.partial(result_kernel, 1.0 / (KX * KY * KZ) ** 0.5),
        [((X, 2 * R, Z, HALF), None), ((3, X), None)],
        [partial2, section, code_p, fields_p, shell_p, up, up2, down2, sums2],
        ops=3_000_000,
    )
    return (state_adjoint, field_grad)


def solution(mesh):
    return jax.shard_map(
        shards,
        mesh=mesh,
        in_specs=(
            P("pos", "ky", "kz", None),
            P("pos", "ky", "kz", None),
            P("pos", "ky", "kz", None),
            P("pos", "ky", "kz", None),
            P(None, "pos"),
            P("ky", "kz", None),
            P("ky", "kz", None),
            P("ky", "kz", None),
            P("ky", "kz", None),
        ),
        out_specs=(P("pos", "ky", "kz", None), P(None, "pos")),
        check_vma=False,
    )
```

```python
import functools

import jax
import jax.numpy as jnp
from jax import lax
from jax.experimental import pallas as pl
from jax.experimental.pallas import tpu as pltpu
from jax.sharding import PartitionSpec as P


KX = 64
KY = 64
KZ = 128
SHELLS = 64
X = 4
R = 8
Z = 16
L = 128
HALF = 64
time_step = 0.25
F32 = jnp.float32
BF16 = jnp.bfloat16
FULL = (X, R, Z, L)
VMEM_LIMIT = 24 * 1024 * 1024


def lanes(shape):
    return lax.broadcasted_iota(jnp.int32, shape, len(shape) - 1)


def pack(low, high):
    return jnp.concatenate([low, high], axis=-1)


def swap(row):
    return pltpu.roll(row, HALF, row.ndim - 1)


def split6(code):
    whole = jnp.floor((code + 0.5) * (1.0 / 6.0))
    return whole, code - 6.0 * whole


def digits_of(code):
    rest, pos = split6(code)
    rest, ky = split6(rest)
    kx, kz = split6(rest)
    return pos, ky, kz, kx


def c_low(digit):
    return jnp.where(digit == 1.0, -0.5, 0.0)


def c_far(digit):
    return jnp.where(digit == 4.0, -0.5, 0.0)


def c_high(digit):
    return jnp.where(digit == 5.0, 0.5, jnp.maximum(0.5 * digit - 0.5, 0.0))


def terms(digit, differ):
    half = -0.5 * differ
    low = jnp.where(digit == 1.0, half, 0.0)
    far = jnp.where(digit == 4.0, half, 0.0)
    high = c_high(digit) * differ
    return low, differ - low - high - far, high, far


def coeffs(digit):
    low, high, far = c_low(digit), c_high(digit), c_far(digit)
    return low, 1.0 - low - high - far, high, far


class Shifts:
    def __init__(self):
        lane = lanes((Z, L))
        self.low = lane < HALF
        kx = lane & (HALF - 1)
        self.kx_first, self.kx_second = kx == 0, kx < 2
        self.kx_last, self.kx_pair = kx == HALF - 1, kx >= HALF - 2
        z = lax.broadcasted_iota(jnp.int32, (Z, L), 0)
        self.z0, self.z1 = z == 0, z == 1
        self.z_last, self.z_before = z == Z - 1, z == Z - 2

    def kx(self, row, by):
        mask, wrapped = {
            -1: (self.kx_last, HALF - 1),
            -2: (self.kx_pair, HALF - 2),
            1: (self.kx_first, HALF + 1),
            2: (self.kx_second, HALF + 2),
        }[by]
        return jnp.where(mask, pltpu.roll(row, wrapped, 1), pltpu.roll(row, by % L, 1))

    def kz_next(self, row, after):
        return jnp.where(self.z_last, after, pltpu.roll(row, Z - 1, 0))

    def kz_next2(self, row, after, after2):
        return jnp.where(self.z_last, after2, jnp.where(self.z_before, after, pltpu.roll(row, Z - 2, 0)))

    def kz_prev(self, row, before):
        return jnp.where(self.z0, before, pltpu.roll(row, 1, 0))

    def kz_prev2(self, row, before, before2):
        return jnp.where(self.z0, before2, jnp.where(self.z1, before, pltpu.roll(row, 2, 0)))


def ky_up_rows(array):
    return array, swap(array)


def ky_down_rows(array):
    return swap(array), array


def along_kx(sh, u, digit):
    low, centre, high, far = terms(digit, u - sh.kx(u, -1))
    return sh.kx(low, -1) + centre + sh.kx(high, 1) + sh.kx(far, 2)


def along_kz(sh, u, digit, above, t_above, digit_b, below, s_below):
    low, centre, high, far = terms(digit, u - sh.kz_next(u, above))
    edge = below - u[0:1]
    return (
        sh.kz_next(low, t_above)
        + centre
        + sh.kz_prev(high, c_high(digit_b) * edge)
        + sh.kz_prev2(far, c_far(digit_b) * edge, s_below)
    )


def along_ky(sh, rows, digit_rows, above, t_above, digit_b, below, s_below):
    nxt = rows[1:] + [jnp.where(sh.low, swap(rows[0]), above)]
    parts = [terms(digit_rows[r], rows[r] - nxt[r]) for r in range(R)]
    edge = below - rows[0]
    low_after = jnp.where(sh.low, swap(parts[0][0]), t_above)
    high_before = jnp.where(sh.low, c_high(digit_b) * edge, swap(parts[R - 1][2]))
    far_before = jnp.where(sh.low, c_far(digit_b) * edge, swap(parts[R - 1][3]))
    far_before2 = jnp.where(sh.low, s_below, swap(parts[R - 2][3]))
    lows = [p[0] for p in parts] + [low_after]
    highs = [high_before] + [p[2] for p in parts]
    fars = [far_before2, far_before] + [p[3] for p in parts]
    return [lows[r + 1] + parts[r][1] + highs[r] + fars[r] for r in range(R)]


def gather(table, index):
    wide = jnp.broadcast_to(table, (Z, L))
    return jnp.take_along_axis(wide, index, axis=1)


def pos_terms(rows, digit_rows):
    nxt = rows[1:] + [None]
    parts = [
        terms(digit_rows[x], rows[x] - nxt[x] if nxt[x] is not None else rows[x])
        for x in range(X)
    ]
    out = []
    for x in range(X):
        value = parts[x][1]
        if x + 1 < X:
            value = value + parts[x + 1][0]
        if x >= 1:
            value = value + parts[x - 1][2]
        if x >= 2:
            value = value + parts[x - 2][3]
        out.append(value)
    return out


def pos_corrections(first, digit_last, digit_b, below, s_below, above, t_above):
    edge = below - first
    low, centre, _, _ = coeffs(digit_last)
    return (
        c_high(digit_b) * edge + s_below,
        c_far(digit_b) * edge,
        -low * above,
        t_above - centre * above,
    )


def shell_sums(w_ref, shell_ref):
    shells = lax.broadcasted_iota(jnp.int32, (SHELLS, L), 0)

    def body(r, total):
        left = jnp.concatenate(
            [w_ref[r, pl.ds(z, 2 * X, stride=Z), :] for z in range(Z)], axis=1
        ).astype(BF16)
        right = jnp.concatenate(
            [
                jnp.where(shells == shell_ref[r, z : z + 1, :], 1.0, 0.0).astype(BF16)
                for z in range(Z)
            ],
            axis=1,
        )
        return total + lax.dot_general(
            left, right, (((1,), (1,)), ((), ())), preferred_element_type=F32
        )

    both = lax.fori_loop(0, R, body, jnp.zeros((2 * X, SHELLS), F32))
    return both[:X] + both[X:]


def put_weighted(w_ref, r, x, value):
    head = value.astype(BF16).astype(F32)
    w_ref[r, x * Z : (x + 1) * Z, :] = head
    w_ref[r, (X + x) * Z : (X + x + 1) * Z, :] = value - head


def edges_kernel(
    u_hbm, code_hbm, start_hbm, vel_hbm, pos_up, pos_down, ky_up, ky_down, kz_up, kz_down,
    u_ref, code_ref, start_ref, vel_ref, arrived,
):
    pairs = ((u_hbm, u_ref), (code_hbm, code_ref), (vel_hbm, vel_ref), (start_hbm, start_ref))
    copies = [pltpu.make_async_copy(a, b, arrived.at[n]) for n, (a, b) in enumerate(pairs)]
    for copy in copies:
        copy.start()
    for copy in copies[:3]:
        copy.wait()

    def whole(ref, x, r):
        return pack(ref[x, r], ref[x, r + R])

    def plane(ref, x, z):
        both = ref[x, :, z, :]
        return pack(both[:R], both[R:])

    for r in range(R):
        v = pack(vel_ref[r], vel_ref[r + R])
        u0, u1, u2, u3 = (v * whole(u_ref, x, r) for x in range(X))
        d0, d2, d3 = (split6(whole(code_ref, x, r).astype(F32))[1] for x in (0, 2, 3))
        pos_up[0, r] = d3
        pos_up[1, r] = u3
        pos_up[2, r] = c_far(d2) * (u2 - u3)
        pos_down[0, r] = u0
        pos_down[1, r] = c_low(d0) * (u0 - u1)
    copies[3].wait()
    for x in range(X):
        k = 2 * R - 1
        d_last = digits_of(code_ref[x, k].astype(F32))[1]
        d_prev = digits_of(code_ref[x, k - 1].astype(F32))[1]
        last, prev = u_ref[x, k], u_ref[x, k - 1]
        ky_up[0, x] = pack(d_last, last)
        ky_up[1, x] = pack(c_far(d_prev) * (prev - last), start_ref[x, k])
        ky_up[2, x] = pack(start_ref[x, k - 1], start_ref[x, k - 1])
        d_first = digits_of(code_ref[x, 0].astype(F32))[1]
        first, second = u_ref[x, 0], u_ref[x, 1]
        ky_down[0, x] = pack(first, c_low(d_first) * (first - second))
        ky_down[1, x] = pack(start_ref[x, 0], start_ref[x, 1])
        d_last = digits_of(plane(code_ref, x, Z - 1).astype(F32))[2]
        d_prev = digits_of(plane(code_ref, x, Z - 2).astype(F32))[2]
        last, prev = plane(u_ref, x, Z - 1), plane(u_ref, x, Z - 2)
        kz_up[0, x] = d_last
        kz_up[1, x] = last
        kz_up[2, x] = c_far(d_prev) * (prev - last)
        kz_up[3, x] = plane(start_ref, x, Z - 1)
        kz_up[4, x] = plane(start_ref, x, Z - 2)
        d_first = digits_of(plane(code_ref, x, 0).astype(F32))[2]
        first, second = plane(u_ref, x, 0), plane(u_ref, x, 1)
        kz_down[0, x] = first
        kz_down[1, x] = c_low(d_first) * (first - second)
        kz_down[2, x] = plane(start_ref, x, 0)
        kz_down[3, x] = plane(start_ref, x, 1)


def first_sums_kernel(
    field, u_ref, code_ref, vel_ref, shell_ref, out_ref, in_ref, section_ref, start_ref,
    u_p, code_p, fields_p, shell_p, field_p, section_p, start_p, sums, w_ref,
):
    for c in range(3):
        for x in range(X):
            field_p[c, x] = jnp.broadcast_to(field[c : c + 1, x : x + 1], (R, L))
    for r in range(R):
        fields_p[0, r] = pack(vel_ref[r], vel_ref[r + R])
        weight = pack(out_ref[r], out_ref[r + R])
        fields_p[1, r] = weight
        fields_p[2, r] = pack(in_ref[r], in_ref[r + R])
        shell_p[r] = pack(shell_ref[r], shell_ref[r + R])
        for x in range(X):
            u = pack(u_ref[x, r], u_ref[x, r + R])
            u_p[x, r] = u
            code_p[x, r] = pack(code_ref[x, r], code_ref[x, r + R]).astype(F32)
            section_p[x, r] = pack(section_ref[x, r], section_ref[x, r + R])
            start_p[x, r] = pack(start_ref[x, r], start_ref[x, r + R])
            put_weighted(w_ref, r, x, weight * u)
    totals = shell_sums(w_ref, shell_p)
    tile = jnp.concatenate([totals, jnp.zeros_like(totals)], axis=1)
    for n in range(sums.shape[0]):
        sums[n] = tile


def add_copies(got):
    total = got[0]
    for n in range(1, got.shape[0]):
        total = total + got[n]
    return total


def momentum_terms(sh, field, x, u, digit, k_ky, kz_rows):
    ks = (along_kx(sh, u, digit[3]), k_ky, along_kz(sh, u, digit[2], *kz_rows))
    return ks, sum(field[c, x, 0:1, :] * ks[c] for c in range(3))


def face(digit, f_prev, f, f_next, f_next2):
    low, centre, high, far = coeffs(digit)
    return low * f_prev + centre * f + high * f_next + far * f_next2


def section_kernel(
    field, u_p, code_p, fields_p, section_p, start_p,
    ky_up, ky_down, kz_up, kz_down,
    partial, slopes,
):
    sh = Shifts()

    def body(x, carry):
        rows = [u_p[x, r] for r in range(R)]
        digit = [digits_of(code_p[x, r]) for r in range(R)]
        start = [start_p[x, r] for r in range(R)]
        d_b, below = ky_up_rows(ky_up[0, x])
        s_below, f_below = ky_up_rows(ky_up[1, x])
        f_below2 = ky_up[2, x]
        above, t_above = ky_down_rows(ky_down[0, x])
        f_above, f_above2 = ky_down_rows(ky_down[1, x])
        k_ky = along_ky(sh, rows, [d[1] for d in digit], above, t_above, d_b, below, s_below)
        before = [jnp.where(sh.low, f_below, swap(start[R - 1]))] + start[:-1]
        after = start + [
            jnp.where(sh.low, swap(start[0]), f_above),
            jnp.where(sh.low, swap(start[1]), f_above2),
        ]
        faces = [face(digit[r][1], before[r], start[r], after[r + 1], after[r + 2]) for r in range(R)]
        face_b = face(d_b, f_below2, f_below, start[0], start[1])
        faces_before = [jnp.where(sh.low, face_b, swap(faces[R - 1]))] + faces[:-1]
        grad_x = [jnp.zeros((Z, L), F32)] * 3
        for r in range(R):
            u, f, d = rows[r], start[r], digit[r]
            up = [kz_up[n, x, r : r + 1, :] for n in range(5)]
            down = [kz_down[n, x, r : r + 1, :] for n in range(4)]
            ks, push = momentum_terms(sh, field, x, u, d, k_ky[r], (down[0], down[1], up[0], up[1], up[2]))
            grad_x = [g + section_p[x, r] * k for g, k in zip(grad_x, ks)]
            partial[x, r] = push
            faces_kx = face(d[3], sh.kx(f, 1), f, sh.kx(f, -1), sh.kx(f, -2))
            slopes[0, x, r] = faces_kx - sh.kx(faces_kx, 1)
            slopes[1, x, r] = faces[r] - faces_before[r]
            faces_kz = face(
                d[2], sh.kz_prev(f, up[3]), f, sh.kz_next(f, down[2]), sh.kz_next2(f, down[2], down[3])
            )
            slopes[2, x, r] = faces_kz - sh.kz_prev(faces_kz, face(up[0], up[4], up[3], f[0:1], f[1:2]))
        for c in range(3):
            slopes[c, x, R] = grad_x[c]
        return carry

    lax.fori_loop(0, X, body, 0)

    def finish(r, carry):
        v = fields_p[0, r]
        us = [u_p[x, r] for x in range(X)]
        k_pos = pos_terms([v * u for u in us], [split6(code_p[x, r])[1] for x in range(X)])
        for x in range(X):
            partial[x, r] = 0.5 * us[x] - (0.5 * time_step) * (partial[x, r] + k_pos[x] + us[x])
        return carry

    lax.fori_loop(0, R, finish, 0)


def section_edges_kernel(
    partial, u_p, code_p, fields_p, shell_p, got_up, got_down, got_sums, section, pos_up, pos_down
):
    totals = add_copies(got_sums)

    def body(r, carry):
        v, back, shell = fields_p[0, r], fields_p[2, r], shell_p[r]
        d0, d2, d3 = (split6(code_p[x, r])[1] for x in (0, 2, 3))
        more = pos_corrections(
            v * u_p[0, r], d3, got_up[0, r], got_up[1, r], got_up[2, r], got_down[0, r], got_down[1, r]
        )
        m = []
        for x in range(X):
            value = partial[x, r] + (0.5 * time_step) * (back * gather(totals[x : x + 1], shell) - more[x])
            section[x, r] = value
            m.append(v * value)
        pos_up[0, r] = m[3]
        pos_up[1, r] = c_far(d2) * (m[2] - m[3])
        pos_down[0, r] = m[0]
        pos_down[1, r] = c_low(d0) * (m[0] - m[1])
        return carry

    lax.fori_loop(0, R, body, 0)


def momentum_edges_kernel(section, code_p, ky_up, ky_down, kz_up, kz_down):
    low_half = lanes((Z, L)) < HALF
    for x in range(X):
        last, prev = section[x, R - 1], section[x, R - 2]
        far = c_far(digits_of(code_p[x, R - 2])[1]) * (prev - last)
        ky_up[x] = jnp.where(low_half, swap(last), far)
        first, second = section[x, 0], section[x, 1]
        low = c_low(digits_of(code_p[x, 0])[1]) * (first - second)
        ky_down[x] = jnp.where(low_half, first, swap(low))
        last, prev = section[x, :, Z - 1, :], section[x, :, Z - 2, :]
        kz_up[0, x] = last
        kz_up[1, x] = c_far(digits_of(code_p[x, :, Z - 2, :])[2]) * (prev - last)
        first, second = section[x, :, 0, :], section[x, :, 1, :]
        kz_down[0, x] = first
        kz_down[1, x] = c_low(digits_of(code_p[x, :, 0, :])[2]) * (first - second)


def second_sums_kernel(section, fields_p, shell_p, slopes, sums, w_ref):
    row = lax.broadcasted_iota(jnp.int32, (X, SHELLS), 0)
    column = lax.broadcasted_iota(jnp.int32, (X, SHELLS), 1)
    inner = jnp.zeros((X, SHELLS), F32)
    for x in range(X):
        parts = [(0.5 * time_step) * slopes[c, x, R] for c in range(3)]
        for r in range(R):
            value = section[x, r]
            put_weighted(w_ref, r, x, fields_p[1, r] * value)
            parts = [p + time_step * (value * slopes[c, x, r]) for c, p in enumerate(parts)]
        for c in range(3):
            whole = jnp.sum(jnp.sum(parts[c], axis=0, keepdims=True), axis=1, keepdims=True)
            inner = inner - jnp.where((row == x) & (column == c), whole, 0.0)
    tile = jnp.concatenate([shell_sums(w_ref, shell_p), inner], axis=1)
    for n in range(sums.shape[0]):
        sums[n] = tile


def interior_kernel(field, section, u_p, code_p, fields_p, first_up, first_kz, ky_up, ky_down, kz_up, kz_down, partial):
    sh = Shifts()

    def body(x, carry):
        rows = [section[x, r] for r in range(R)]
        digit = [digits_of(code_p[x, r]) for r in range(R)]
        below, s_below = ky_up_rows(ky_up[x])
        above, t_above = ky_down_rows(ky_down[x])
        k_ky = along_ky(sh, rows, [d[1] for d in digit], above, t_above, first_up[0, x], below, s_below)
        for r in range(R):
            here = slice(r, r + 1)
            kz_rows = (
                kz_down[0, x, here, :],
                kz_down[1, x, here, :],
                first_kz[0, x, here, :],
                kz_up[0, x, here, :],
                kz_up[1, x, here, :],
            )
            _, push = momentum_terms(sh, field, x, rows[r], digit[r], k_ky[r], kz_rows)
            partial[x, r] = push
        return carry

    lax.fori_loop(0, X, body, 0)

    def finish(r, carry):
        v = fields_p[0, r]
        ms = [section[x, r] for x in range(X)]
        k_pos = pos_terms([v * m for m in ms], [split6(code_p[x, r])[1] for x in range(X)])
        for x in range(X):
            partial[x, r] = (
                0.5 * u_p[x, r] + ms[x] - time_step * (partial[x, r] + k_pos[x] + ms[x])
            )
        return carry

    lax.fori_loop(0, R, finish, 0)


def result_kernel(
    scale, partial, section, code_p, fields_p, shell_p, first_up, got_up, got_down, got_sums, state, grad
):
    totals = add_copies(got_sums)
    for r in range(R):
        v, back, shell = fields_p[0, r], fields_p[2, r], shell_p[r]
        more = pos_corrections(
            v * section[0, r], split6(code_p[3, r])[1], first_up[0, r], got_up[0, r], got_up[1, r],
            got_down[0, r], got_down[1, r],
        )
        for x in range(X):
            value = partial[x, r] + time_step * (back * gather(totals[x : x + 1], shell) - more[x])
            state[x, r] = value[:, :HALF]
            state[x, r + R] = value[:, HALF:]
    row = lax.broadcasted_iota(jnp.int32, (X, L), 0)
    column = lanes((X, L))
    for c in range(3):
        spread = jnp.broadcast_to(totals[:, SHELLS + c : SHELLS + c + 1], (X, L))
        line = jnp.sum(jnp.where(row == column, spread, 0.0), axis=0, keepdims=True)
        grad[c : c + 1, :] = line[:, :X] * scale


def call(kernel, outs, args, in_hbm=False, scratch=(), ops=0, aliases={}):
    if in_hbm:
        args = [pltpu.with_memory_space_constraint(a, pltpu.HBM) for a in args]
    shapes = [jax.ShapeDtypeStruct(shape, F32 if dtype is None else dtype) for shape, dtype in outs]
    moved = sum(4 * a.size for a in args) + sum(4 * s.size for s in shapes)
    vmem = pl.BlockSpec(memory_space=pltpu.VMEM)
    given = pl.BlockSpec(memory_space=pltpu.HBM) if in_hbm else vmem
    return pl.pallas_call(
        kernel,
        out_shape=shapes,
        in_specs=[given] * len(args),
        out_specs=[vmem] * len(shapes),
        scratch_shapes=list(scratch),
        input_output_aliases=aliases,
        compiler_params=pltpu.CompilerParams(vmem_limit_bytes=VMEM_LIMIT),
        cost_estimate=pl.CostEstimate(flops=ops, bytes_accessed=moved, transcendentals=0),
    )(*args)


def shift(array, axis, by, wrap=True):
    count = lax.axis_size(axis)
    pairs = [(i, (i + by) % count) for i in range(count) if wrap or 0 <= i + by < count]
    return lax.ppermute(array, axis, pairs)


def shift_both(up, down, axis, wrap=True):
    up = shift(up, axis, 1, wrap)
    down = shift(down, axis, -1, wrap)
    return up, down


def exchange(copies):
    return lax.all_to_all(copies, ("ky", "kz"), 0, 0)


def shards(
    cotangent,
    start_state,
    section_state,
    face_codes,
    field_strength,
    velocity,
    shell_index,
    shell_out,
    shell_in,
):
    members = lax.axis_size("ky") * lax.axis_size("kz")
    plane, ky_plane, kz_plane = (R, Z, L), (X, Z, L), (X, R, L)
    w_scratch = [pltpu.VMEM((R, 2 * X * Z, L), F32)]
    sums_shape = ((members, X, L), None)
    up, down, ky_up, ky_down, kz_up, kz_down, u_v, code_v, start_v, vel_v = call(
        edges_kernel,
        [((3,) + plane, None), ((2,) + plane, None), ((3,) + ky_plane, None), ((2,) + ky_plane, None),
         ((5,) + kz_plane, None), ((4,) + kz_plane, None), (cotangent.shape, None), (cotangent.shape, jnp.int32),
         (cotangent.shape, None), (velocity.shape, None)],
        [cotangent, face_codes, start_state, velocity],
        in_hbm=True,
        scratch=[pltpu.SemaphoreType.DMA((4,))],
        ops=4_000_000,
    )
    up, down = shift_both(up, down, "pos", False)
    ky_up, ky_down = shift_both(ky_up, ky_down, "ky")
    kz_up, kz_down = shift_both(kz_up, kz_down, "kz")
    u_p, code_p, fields_p, shell_p, field_p, section_p, start_p, sums = call(
        first_sums_kernel,
        [(FULL, None), (FULL, None), ((3,) + plane, None), (plane, jnp.int32), ((3, X, R, L), None),
         (FULL, None), (FULL, None), sums_shape],
        [field_strength, u_v, code_v, vel_v, shell_index, shell_out, shell_in, section_state, start_v],
        scratch=w_scratch,
        ops=8_000_000,
    )
    sums = exchange(sums)
    partial, slopes = call(
        section_kernel,
        [(FULL, None), ((3, X, R + 1, Z, L), None)],
        [field_p, u_p, code_p, fields_p, section_p, start_p, ky_up, ky_down, kz_up, kz_down],
        ops=16_000_000,
    )
    section, up2, down2 = call(
        section_edges_kernel,
        [(FULL, None), ((2,) + plane, None), ((2,) + plane, None)],
        [partial, u_p, code_p, fields_p, shell_p, up, down, sums],
        aliases={0: 0},
        ops=2_000_000,
    )
    up2, down2 = shift_both(up2, down2, "pos", False)
    ky_up2, ky_down2, kz_up2, kz_down2 = call(
        momentum_edges_kernel,
        [(ky_plane, None), (ky_plane, None), ((2,) + kz_plane, None), ((2,) + kz_plane, None)],
        [section, code_p],
        ops=1_000_000,
    )
    ky_up2, ky_down2 = shift_both(ky_up2, ky_down2, "ky")
    kz_up2, kz_down2 = shift_both(kz_up2, kz_down2, "kz")
    (sums2,) = call(
        second_sums_kernel, [sums_shape], [section, fields_p, shell_p, slopes], scratch=w_scratch, ops=4_000_000
    )
    sums2 = exchange(sums2)
    (partial2,) = call(
        interior_kernel,
        [(FULL, None)],
        [field_p, section, u_p, code_p, fields_p, ky_up, kz_up, ky_up2, ky_down2, kz_up2, kz_down2],
        ops=8_000_000,
    )
    state_adjoint, field_grad = call(
        functools.partial(result_kernel, 1.0 / (KX * KY * KZ) ** 0.5),
        [((X, 2 * R, Z, HALF), None), ((3, X), None)],
        [partial2, section, code_p, fields_p, shell_p, up, up2, down2, sums2],
        ops=3_000_000,
    )
    return (state_adjoint, field_grad)


def solution(mesh):
    return jax.shard_map(
        shards,
        mesh=mesh,
        in_specs=(
            P("pos", "ky", "kz", None),
            P("pos", "ky", "kz", None),
            P("pos", "ky", "kz", None),
            P("pos", "ky", "kz", None),
            P(None, "pos"),
            P("ky", "kz", None),
            P("ky", "kz", None),
            P("ky", "kz", None),
            P("ky", "kz", None),
        ),
        out_specs=(P("pos", "ky", "kz", None), P(None, "pos")),
        check_vma=False,
    )
```

```python
import functools

import jax
import jax.numpy as jnp
from jax import lax
from jax.experimental import pallas as pl
from jax.experimental.pallas import tpu as pltpu
from jax.sharding import PartitionSpec as P


KX = 64
KY = 64
KZ = 128
SHELLS = 64
X = 4
R = 8
Z = 16
L = 128
HALF = 64
time_step = 0.25
F32 = jnp.float32
BF16 = jnp.bfloat16
FULL = (X, R, Z, L)
VMEM_LIMIT = 24 * 1024 * 1024


def lanes(shape):
    return lax.broadcasted_iota(jnp.int32, shape, len(shape) - 1)


def pack(low, high):
    return jnp.concatenate([low, high], axis=-1)


def swap(row):
    return pltpu.roll(row, HALF, row.ndim - 1)


def split6(code):
    whole = jnp.floor((code + 0.5) * (1.0 / 6.0))
    return whole, code - 6.0 * whole


def digits_of(code):
    rest, pos = split6(code)
    rest, ky = split6(rest)
    kx, kz = split6(rest)
    return pos, ky, kz, kx


def c_low(digit):
    return jnp.where(digit == 1.0, -0.5, 0.0)


def c_far(digit):
    return jnp.where(digit == 4.0, -0.5, 0.0)


def c_high(digit):
    return jnp.where(digit == 5.0, 0.5, jnp.maximum(0.5 * digit - 0.5, 0.0))


def terms(digit, differ):
    half = -0.5 * differ
    low = jnp.where(digit == 1.0, half, 0.0)
    far = jnp.where(digit == 4.0, half, 0.0)
    high = c_high(digit) * differ
    return low, differ - low - high - far, high, far


def coeffs(digit):
    low, high, far = c_low(digit), c_high(digit), c_far(digit)
    return low, 1.0 - low - high - far, high, far


class Shifts:
    def __init__(self):
        lane = lanes((Z, L))
        self.low = lane < HALF
        self.moved = {by: (lane & HALF) | ((lane - by) & (HALF - 1)) for by in (-2, -1, 1, 2)}
        z = lax.broadcasted_iota(jnp.int32, (Z, L), 0)
        self.z0, self.z1 = z == 0, z == 1
        self.z_last, self.z_before = z == Z - 1, z == Z - 2

    def kx(self, row, by):
        return jnp.take_along_axis(row, self.moved[by], axis=1)

    def kz_next(self, row, after):
        return jnp.where(self.z_last, after, pltpu.roll(row, Z - 1, 0))

    def kz_next2(self, row, after, after2):
        return jnp.where(self.z_last, after2, jnp.where(self.z_before, after, pltpu.roll(row, Z - 2, 0)))

    def kz_prev(self, row, before):
        return jnp.where(self.z0, before, pltpu.roll(row, 1, 0))

    def kz_prev2(self, row, before, before2):
        return jnp.where(self.z0, before2, jnp.where(self.z1, before, pltpu.roll(row, 2, 0)))


def ky_up_rows(array):
    return array, swap(array)


def ky_down_rows(array):
    return swap(array), array


def along_kx(sh, u, digit):
    low, centre, high, far = terms(digit, u - sh.kx(u, -1))
    return sh.kx(low, -1) + centre + sh.kx(high + sh.kx(far, 1), 1)


def along_kz(sh, u, digit, above, t_above, digit_b, below, s_below):
    low, centre, high, far = terms(digit, u - sh.kz_next(u, above))
    edge = below - u[0:1]
    far = sh.kz_prev(far, c_far(digit_b) * edge)
    return sh.kz_next(low, t_above) + centre + sh.kz_prev(high + far, c_high(digit_b) * edge + s_below)


def along_ky(sh, rows, digit_rows, above, t_above, digit_b, below, s_below):
    nxt = rows[1:] + [jnp.where(sh.low, swap(rows[0]), above)]
    parts = [terms(digit_rows[r], rows[r] - nxt[r]) for r in range(R)]
    edge = below - rows[0]
    low_after = jnp.where(sh.low, swap(parts[0][0]), t_above)
    high_before = jnp.where(sh.low, c_high(digit_b) * edge, swap(parts[R - 1][2]))
    far_before = jnp.where(sh.low, c_far(digit_b) * edge, swap(parts[R - 1][3]))
    far_before2 = jnp.where(sh.low, s_below, swap(parts[R - 2][3]))
    lows = [p[0] for p in parts] + [low_after]
    highs = [high_before] + [p[2] for p in parts]
    fars = [far_before2, far_before] + [p[3] for p in parts]
    return [lows[r + 1] + parts[r][1] + highs[r] + fars[r] for r in range(R)]


def gather(table, index):
    wide = jnp.broadcast_to(table, (Z, L))
    return jnp.take_along_axis(wide, index, axis=1)


def pos_terms(rows, digit_rows):
    nxt = rows[1:] + [None]
    parts = [
        terms(digit_rows[x], rows[x] - nxt[x] if nxt[x] is not None else rows[x])
        for x in range(X)
    ]
    out = []
    for x in range(X):
        value = parts[x][1]
        if x + 1 < X:
            value = value + parts[x + 1][0]
        if x >= 1:
            value = value + parts[x - 1][2]
        if x >= 2:
            value = value + parts[x - 2][3]
        out.append(value)
    return out


def pos_corrections(first, digit_last, digit_b, below, s_below, above, t_above):
    edge = below - first
    low, centre, _, _ = coeffs(digit_last)
    return (
        c_high(digit_b) * edge + s_below,
        c_far(digit_b) * edge,
        -low * above,
        t_above - centre * above,
    )


def shell_sums(w_ref, shell_ref):
    shells = lax.broadcasted_iota(jnp.int32, (SHELLS, L), 0)

    def body(r, total):
        left = jnp.concatenate(
            [w_ref[r, pl.ds(z, 2 * X, stride=Z), :] for z in range(Z)], axis=1
        ).astype(BF16)
        right = jnp.concatenate(
            [
                jnp.where(shells == shell_ref[r, z : z + 1, :], 1.0, 0.0).astype(BF16)
                for z in range(Z)
            ],
            axis=1,
        )
        return total + lax.dot_general(
            left, right, (((1,), (1,)), ((), ())), preferred_element_type=F32
        )

    both = jnp.zeros((2 * X, SHELLS), F32)
    for r in range(R):
        both = body(r, both)
    return both[:X] + both[X:]


def put_weighted(w_ref, r, x, value):
    head = value.astype(BF16).astype(F32)
    w_ref[r, x * Z : (x + 1) * Z, :] = head
    w_ref[r, (X + x) * Z : (X + x + 1) * Z, :] = value - head


def edges_kernel(
    u_hbm, code_hbm, start_hbm, vel_hbm, field_hbm, pos_up, pos_down, ky_up, ky_down, kz_up, kz_down,
    u_ref, code_ref, start_ref, vel_ref, field_ref, arrived,
):
    pairs = ((u_hbm, u_ref), (code_hbm, code_ref), (vel_hbm, vel_ref), (start_hbm, start_ref), (field_hbm, field_ref))
    copies = [pltpu.make_async_copy(a, b, arrived.at[n]) for n, (a, b) in enumerate(pairs)]
    for copy in copies:
        copy.start()
    for copy in copies[:3]:
        copy.wait()

    def whole(ref, x, r):
        return pack(ref[x, r], ref[x, r + R])

    def plane(ref, x, z):
        both = ref[x, :, z, :]
        return pack(both[:R], both[R:])

    for r in range(R):
        v = pack(vel_ref[r], vel_ref[r + R])
        u0, u1, u2, u3 = (v * whole(u_ref, x, r) for x in range(X))
        d0, d2, d3 = (split6(whole(code_ref, x, r).astype(F32))[1] for x in (0, 2, 3))
        pos_up[0, r] = d3
        pos_up[1, r] = u3
        pos_up[2, r] = c_far(d2) * (u2 - u3)
        pos_down[0, r] = u0
        pos_down[1, r] = c_low(d0) * (u0 - u1)
    copies[3].wait()
    for x in range(X):
        k = 2 * R - 1
        d_last = digits_of(code_ref[x, k].astype(F32))[1]
        d_prev = digits_of(code_ref[x, k - 1].astype(F32))[1]
        last, prev = u_ref[x, k], u_ref[x, k - 1]
        ky_up[0, x] = pack(d_last, last)
        ky_up[1, x] = pack(c_far(d_prev) * (prev - last), start_ref[x, k])
        ky_up[2, x] = pack(start_ref[x, k - 1], start_ref[x, k - 1])
        d_first = digits_of(code_ref[x, 0].astype(F32))[1]
        first, second = u_ref[x, 0], u_ref[x, 1]
        ky_down[0, x] = pack(first, c_low(d_first) * (first - second))
        ky_down[1, x] = pack(start_ref[x, 0], start_ref[x, 1])
        d_last = digits_of(plane(code_ref, x, Z - 1).astype(F32))[2]
        d_prev = digits_of(plane(code_ref, x, Z - 2).astype(F32))[2]
        last, prev = plane(u_ref, x, Z - 1), plane(u_ref, x, Z - 2)
        kz_up[0, x] = d_last
        kz_up[1, x] = last
        kz_up[2, x] = c_far(d_prev) * (prev - last)
        kz_up[3, x] = plane(start_ref, x, Z - 1)
        kz_up[4, x] = plane(start_ref, x, Z - 2)
        d_first = digits_of(plane(code_ref, x, 0).astype(F32))[2]
        first, second = plane(u_ref, x, 0), plane(u_ref, x, 1)
        kz_down[0, x] = first
        kz_down[1, x] = c_low(d_first) * (first - second)
        kz_down[2, x] = plane(start_ref, x, 0)
        kz_down[3, x] = plane(start_ref, x, 1)
    copies[4].wait()


def first_sums_kernel(
    field, u_ref, code_ref, vel_ref, shell_ref, out_ref, in_ref, section_ref, start_ref,
    u_p, code_p, fields_p, shell_p, field_p, section_p, start_p, sums, w_ref,
):
    for c in range(3):
        for x in range(X):
            field_p[c, x] = jnp.broadcast_to(field[c : c + 1, x : x + 1], (R, L))
    for r in range(R):
        fields_p[0, r] = pack(vel_ref[r], vel_ref[r + R])
        weight = pack(out_ref[r], out_ref[r + R])
        fields_p[1, r] = weight
        fields_p[2, r] = pack(in_ref[r], in_ref[r + R])
        shell_p[r] = pack(shell_ref[r], shell_ref[r + R])
        for x in range(X):
            u = pack(u_ref[x, r], u_ref[x, r + R])
            u_p[x, r] = u
            code_p[x, r] = pack(code_ref[x, r], code_ref[x, r + R]).astype(F32)
            section_p[x, r] = pack(section_ref[x, r], section_ref[x, r + R])
            start_p[x, r] = pack(start_ref[x, r], start_ref[x, r + R])
            put_weighted(w_ref, r, x, weight * u)
    totals = shell_sums(w_ref, shell_p)
    tile = jnp.concatenate([totals, jnp.zeros_like(totals)], axis=1)
    for n in range(sums.shape[0]):
        sums[n] = tile


def add_copies(got):
    total = got[0]
    for n in range(1, got.shape[0]):
        total = total + got[n]
    return total


def momentum_terms(sh, field, x, u, digit, k_ky, kz_rows):
    ks = (along_kx(sh, u, digit[3]), k_ky, along_kz(sh, u, digit[2], *kz_rows))
    return ks, sum(field[c, x, 0:1, :] * ks[c] for c in range(3))


def face(digit, f_prev, f, f_next, f_next2):
    low, centre, high, far = coeffs(digit)
    return low * f_prev + centre * f + high * f_next + far * f_next2


def section_kernel(
    field, u_p, code_p, fields_p, section_p, start_p,
    ky_up, ky_down, kz_up, kz_down,
    partial, slopes,
):
    sh = Shifts()

    def body(x, carry):
        rows = [u_p[x, r] for r in range(R)]
        digit = [digits_of(code_p[x, r]) for r in range(R)]
        start = [start_p[x, r] for r in range(R)]
        d_b, below = ky_up_rows(ky_up[0, x])
        s_below, f_below = ky_up_rows(ky_up[1, x])
        f_below2 = ky_up[2, x]
        above, t_above = ky_down_rows(ky_down[0, x])
        f_above, f_above2 = ky_down_rows(ky_down[1, x])
        k_ky = along_ky(sh, rows, [d[1] for d in digit], above, t_above, d_b, below, s_below)
        before = [jnp.where(sh.low, f_below, swap(start[R - 1]))] + start[:-1]
        after = start + [
            jnp.where(sh.low, swap(start[0]), f_above),
            jnp.where(sh.low, swap(start[1]), f_above2),
        ]
        faces = [face(digit[r][1], before[r], start[r], after[r + 1], after[r + 2]) for r in range(R)]
        face_b = face(d_b, f_below2, f_below, start[0], start[1])
        faces_before = [jnp.where(sh.low, face_b, swap(faces[R - 1]))] + faces[:-1]
        grad_x = [jnp.zeros((Z, L), F32)] * 3
        for r in range(R):
            u, f, d = rows[r], start[r], digit[r]
            up = [kz_up[n, x, r : r + 1, :] for n in range(5)]
            down = [kz_down[n, x, r : r + 1, :] for n in range(4)]
            ks, push = momentum_terms(sh, field, x, u, d, k_ky[r], (down[0], down[1], up[0], up[1], up[2]))
            grad_x = [g + section_p[x, r] * k for g, k in zip(grad_x, ks)]
            partial[x, r] = push
            faces_kx = face(d[3], sh.kx(f, 1), f, sh.kx(f, -1), sh.kx(f, -2))
            slopes[0, x, r] = faces_kx - sh.kx(faces_kx, 1)
            slopes[1, x, r] = faces[r] - faces_before[r]
            faces_kz = face(
                d[2], sh.kz_prev(f, up[3]), f, sh.kz_next(f, down[2]), sh.kz_next2(f, down[2], down[3])
            )
            slopes[2, x, r] = faces_kz - sh.kz_prev(faces_kz, face(up[0], up[4], up[3], f[0:1], f[1:2]))
        for c in range(3):
            slopes[c, x, R] = grad_x[c]
        return carry

    lax.fori_loop(0, X, body, 0)

    def finish(r, carry):
        v = fields_p[0, r]
        us = [u_p[x, r] for x in range(X)]
        k_pos = pos_terms([v * u for u in us], [split6(code_p[x, r])[1] for x in range(X)])
        for x in range(X):
            partial[x, r] = 0.5 * us[x] - (0.5 * time_step) * (partial[x, r] + k_pos[x] + us[x])
        return carry

    lax.fori_loop(0, R, finish, 0)


def section_edges_kernel(
    partial, u_p, code_p, fields_p, shell_p, got_up, got_down, got_sums, section, pos_up, pos_down
):
    totals = add_copies(got_sums)

    def body(r, carry):
        v, back, shell = fields_p[0, r], fields_p[2, r], shell_p[r]
        d0, d2, d3 = (split6(code_p[x, r])[1] for x in (0, 2, 3))
        more = pos_corrections(
            v * u_p[0, r], d3, got_up[0, r], got_up[1, r], got_up[2, r], got_down[0, r], got_down[1, r]
        )
        m = []
        for x in range(X):
            value = partial[x, r] + (0.5 * time_step) * (back * gather(totals[x : x + 1], shell) - more[x])
            section[x, r] = value
            m.append(v * value)
        pos_up[0, r] = m[3]
        pos_up[1, r] = c_far(d2) * (m[2] - m[3])
        pos_down[0, r] = m[0]
        pos_down[1, r] = c_low(d0) * (m[0] - m[1])
        return carry

    lax.fori_loop(0, R, body, 0)


def momentum_edges_kernel(section, code_p, ky_up, ky_down, kz_up, kz_down):
    low_half = lanes((Z, L)) < HALF
    for x in range(X):
        last, prev = section[x, R - 1], section[x, R - 2]
        far = c_far(digits_of(code_p[x, R - 2])[1]) * (prev - last)
        ky_up[x] = jnp.where(low_half, swap(last), far)
        first, second = section[x, 0], section[x, 1]
        low = c_low(digits_of(code_p[x, 0])[1]) * (first - second)
        ky_down[x] = jnp.where(low_half, first, swap(low))
        last, prev = section[x, :, Z - 1, :], section[x, :, Z - 2, :]
        kz_up[0, x] = last
        kz_up[1, x] = c_far(digits_of(code_p[x, :, Z - 2, :])[2]) * (prev - last)
        first, second = section[x, :, 0, :], section[x, :, 1, :]
        kz_down[0, x] = first
        kz_down[1, x] = c_low(digits_of(code_p[x, :, 0, :])[2]) * (first - second)


def second_sums_kernel(section, fields_p, shell_p, slopes, sums, w_ref):
    row = lax.broadcasted_iota(jnp.int32, (X, SHELLS), 0)
    column = lax.broadcasted_iota(jnp.int32, (X, SHELLS), 1)
    inner = jnp.zeros((X, SHELLS), F32)
    for x in range(X):
        parts = [(0.5 * time_step) * slopes[c, x, R] for c in range(3)]
        for r in range(R):
            value = section[x, r]
            put_weighted(w_ref, r, x, fields_p[1, r] * value)
            parts = [p + time_step * (value * slopes[c, x, r]) for c, p in enumerate(parts)]
        for c in range(3):
            whole = jnp.sum(jnp.sum(parts[c], axis=0, keepdims=True), axis=1, keepdims=True)
            inner = inner - jnp.where((row == x) & (column == c), whole, 0.0)
    tile = jnp.concatenate([shell_sums(w_ref, shell_p), inner], axis=1)
    for n in range(sums.shape[0]):
        sums[n] = tile


def interior_kernel(field, section, u_p, code_p, fields_p, first_up, first_kz, ky_up, ky_down, kz_up, kz_down, partial):
    sh = Shifts()

    def body(x, carry):
        rows = [section[x, r] for r in range(R)]
        digit = [digits_of(code_p[x, r]) for r in range(R)]
        below, s_below = ky_up_rows(ky_up[x])
        above, t_above = ky_down_rows(ky_down[x])
        k_ky = along_ky(sh, rows, [d[1] for d in digit], above, t_above, first_up[0, x], below, s_below)
        for r in range(R):
            here = slice(r, r + 1)
            kz_rows = (
                kz_down[0, x, here, :],
                kz_down[1, x, here, :],
                first_kz[0, x, here, :],
                kz_up[0, x, here, :],
                kz_up[1, x, here, :],
            )
            _, push = momentum_terms(sh, field, x, rows[r], digit[r], k_ky[r], kz_rows)
            partial[x, r] = push
        return carry

    lax.fori_loop(0, X, body, 0)

    def finish(r, carry):
        v = fields_p[0, r]
        ms = [section[x, r] for x in range(X)]
        k_pos = pos_terms([v * m for m in ms], [split6(code_p[x, r])[1] for x in range(X)])
        for x in range(X):
            partial[x, r] = (
                0.5 * u_p[x, r] + ms[x] - time_step * (partial[x, r] + k_pos[x] + ms[x])
            )
        return carry

    lax.fori_loop(0, R, finish, 0)


def result_kernel(
    scale, partial, section, code_p, fields_p, shell_p, first_up, got_up, got_down, got_sums, state, grad
):
    totals = add_copies(got_sums)
    for r in range(R):
        v, back, shell = fields_p[0, r], fields_p[2, r], shell_p[r]
        more = pos_corrections(
            v * section[0, r], split6(code_p[3, r])[1], first_up[0, r], got_up[0, r], got_up[1, r],
            got_down[0, r], got_down[1, r],
        )
        for x in range(X):
            value = partial[x, r] + time_step * (back * gather(totals[x : x + 1], shell) - more[x])
            state[x, r] = value[:, :HALF]
            state[x, r + R] = value[:, HALF:]
    row = lax.broadcasted_iota(jnp.int32, (X, L), 0)
    column = lanes((X, L))
    for c in range(3):
        spread = jnp.broadcast_to(totals[:, SHELLS + c : SHELLS + c + 1], (X, L))
        line = jnp.sum(jnp.where(row == column, spread, 0.0), axis=0, keepdims=True)
        grad[c : c + 1, :] = line[:, :X] * scale


def call(kernel, outs, args, in_hbm=False, scratch=(), ops=0, aliases={}):
    if in_hbm:
        args = [pltpu.with_memory_space_constraint(a, pltpu.HBM) for a in args]
    shapes = [jax.ShapeDtypeStruct(shape, F32 if dtype is None else dtype) for shape, dtype in outs]
    moved = sum(4 * a.size for a in args) + sum(4 * s.size for s in shapes)
    vmem = pl.BlockSpec(memory_space=pltpu.VMEM)
    given = pl.BlockSpec(memory_space=pltpu.HBM) if in_hbm else vmem
    return pl.pallas_call(
        kernel,
        out_shape=shapes,
        in_specs=[given] * len(args),
        out_specs=[vmem] * len(shapes),
        scratch_shapes=list(scratch),
        input_output_aliases=aliases,
        compiler_params=pltpu.CompilerParams(vmem_limit_bytes=VMEM_LIMIT),
        cost_estimate=pl.CostEstimate(flops=ops, bytes_accessed=moved, transcendentals=0),
    )(*args)


def shift(array, axis, by, wrap=True):
    count = lax.axis_size(axis)
    pairs = [(i, (i + by) % count) for i in range(count) if wrap or 0 <= i + by < count]
    return lax.ppermute(array, axis, pairs)


def shift_both(up, down, axis, wrap=True):
    up = shift(up, axis, 1, wrap)
    down = shift(down, axis, -1, wrap)
    return up, down


def exchange(copies):
    return lax.all_to_all(copies, ("ky", "kz"), 0, 0)


def shards(
    cotangent,
    start_state,
    section_state,
    face_codes,
    field_strength,
    velocity,
    shell_index,
    shell_out,
    shell_in,
):
    members = lax.axis_size("ky") * lax.axis_size("kz")
    plane, ky_plane, kz_plane = (R, Z, L), (X, Z, L), (X, R, L)
    w_scratch = [pltpu.VMEM((R, 2 * X * Z, L), F32)]
    sums_shape = ((members, X, L), None)
    up, down, ky_up, ky_down, kz_up, kz_down, u_v, code_v, start_v, vel_v, field_v = call(
        edges_kernel,
        [((3,) + plane, None), ((2,) + plane, None), ((3,) + ky_plane, None), ((2,) + ky_plane, None),
         ((5,) + kz_plane, None), ((4,) + kz_plane, None), (cotangent.shape, None), (cotangent.shape, jnp.int32),
         (cotangent.shape, None), (velocity.shape, None), (field_strength.shape, None)],
        [cotangent, face_codes, start_state, velocity, field_strength],
        in_hbm=True,
        scratch=[pltpu.SemaphoreType.DMA((5,))],
        ops=4_000_000,
    )
    up, down = shift_both(up, down, "pos", False)
    ky_up, ky_down = shift_both(ky_up, ky_down, "ky")
    kz_up, kz_down = shift_both(kz_up, kz_down, "kz")
    u_p, code_p, fields_p, shell_p, field_p, section_p, start_p, sums = call(
        first_sums_kernel,
        [(FULL, None), (FULL, None), ((3,) + plane, None), (plane, jnp.int32), ((3, X, R, L), None),
         (FULL, None), (FULL, None), sums_shape],
        [field_v, u_v, code_v, vel_v, shell_index, shell_out, shell_in, section_state, start_v],
        scratch=w_scratch,
        ops=8_000_000,
    )
    sums = exchange(sums)
    partial, slopes = call(
        section_kernel,
        [(FULL, None), ((3, X, R + 1, Z, L), None)],
        [field_p, u_p, code_p, fields_p, section_p, start_p, ky_up, ky_down, kz_up, kz_down],
        ops=16_000_000,
    )
    section, up2, down2 = call(
        section_edges_kernel,
        [(FULL, None), ((2,) + plane, None), ((2,) + plane, None)],
        [partial, u_p, code_p, fields_p, shell_p, up, down, sums],
        aliases={0: 0},
        ops=2_000_000,
    )
    up2, down2 = shift_both(up2, down2, "pos", False)
    ky_up2, ky_down2, kz_up2, kz_down2 = call(
        momentum_edges_kernel,
        [(ky_plane, None), (ky_plane, None), ((2,) + kz_plane, None), ((2,) + kz_plane, None)],
        [section, code_p],
        ops=1_000_000,
    )
    ky_up2, ky_down2 = shift_both(ky_up2, ky_down2, "ky")
    kz_up2, kz_down2 = shift_both(kz_up2, kz_down2, "kz")
    (sums2,) = call(
        second_sums_kernel, [sums_shape], [section, fields_p, shell_p, slopes], scratch=w_scratch, ops=4_000_000
    )
    sums2 = exchange(sums2)
    (partial2,) = call(
        interior_kernel,
        [(FULL, None)],
        [field_p, section, u_p, code_p, fields_p, ky_up, kz_up, ky_up2, ky_down2, kz_up2, kz_down2],
        ops=8_000_000,
    )
    state_adjoint, field_grad = call(
        functools.partial(result_kernel, 1.0 / (KX * KY * KZ) ** 0.5),
        [((X, 2 * R, Z, HALF), None), ((3, X), None)],
        [partial2, section, code_p, fields_p, shell_p, up, up2, down2, sums2],
        ops=3_000_000,
    )
    return (state_adjoint, field_grad)


def solution(mesh):
    return jax.shard_map(
        shards,
        mesh=mesh,
        in_specs=(
            P("pos", "ky", "kz", None),
            P("pos", "ky", "kz", None),
            P("pos", "ky", "kz", None),
            P("pos", "ky", "kz", None),
            P(None, "pos"),
            P("ky", "kz", None),
            P("ky", "kz", None),
            P("ky", "kz", None),
            P("ky", "kz", None),
        ),
        out_specs=(P("pos", "ky", "kz", None), P(None, "pos")),
        check_vma=False,
    )
```

```python
import functools

import jax
import jax.numpy as jnp
from jax import lax
from jax.experimental import pallas as pl
from jax.experimental.pallas import tpu as pltpu
from jax.sharding import PartitionSpec as P


KX = 64
KY = 64
KZ = 128
SHELLS = 64
X = 4
R = 8
Z = 16
L = 128
HALF = 64
time_step = 0.25
F32 = jnp.float32
BF16 = jnp.bfloat16
FULL = (X, R, Z, L)
VMEM_LIMIT = 24 * 1024 * 1024


def lanes(shape):
    return lax.broadcasted_iota(jnp.int32, shape, len(shape) - 1)


def pack(low, high):
    return jnp.concatenate([low, high], axis=-1)


def swap(row):
    return pltpu.roll(row, HALF, row.ndim - 1)


def split6(code):
    whole = jnp.floor((code + 0.5) * (1.0 / 6.0))
    return whole, code - 6.0 * whole


def digits_of(code):
    rest, pos = split6(code)
    rest, ky = split6(rest)
    kx, kz = split6(rest)
    return pos, ky, kz, kx


def c_low(digit):
    return jnp.where(digit == 1.0, -0.5, 0.0)


def c_far(digit):
    return jnp.where(digit == 4.0, -0.5, 0.0)


def c_high(digit):
    return jnp.where(digit == 5.0, 0.5, jnp.maximum(0.5 * digit - 0.5, 0.0))


def terms(digit, differ):
    half = -0.5 * differ
    low = jnp.where(digit == 1.0, half, 0.0)
    far = jnp.where(digit == 4.0, half, 0.0)
    high = c_high(digit) * differ
    return low, differ - low - high - far, high, far


def coeffs(digit):
    low, high, far = c_low(digit), c_high(digit), c_far(digit)
    return low, 1.0 - low - high - far, high, far


class Shifts:
    def __init__(self):
        lane = lanes((Z, L))
        self.low = lane < HALF
        self.moved = {by: (lane & HALF) | ((lane - by) & (HALF - 1)) for by in (-2, -1, 1, 2)}
        z = lax.broadcasted_iota(jnp.int32, (Z, L), 0)
        self.z0, self.z1 = z == 0, z == 1
        self.z_last, self.z_before = z == Z - 1, z == Z - 2

    def kx(self, row, by):
        return jnp.take_along_axis(row, self.moved[by], axis=1)

    def kz_next(self, row, after):
        return jnp.where(self.z_last, after, pltpu.roll(row, Z - 1, 0))

    def kz_next2(self, row, after, after2):
        return jnp.where(self.z_last, after2, jnp.where(self.z_before, after, pltpu.roll(row, Z - 2, 0)))

    def kz_prev(self, row, before):
        return jnp.where(self.z0, before, pltpu.roll(row, 1, 0))

    def kz_prev2(self, row, before, before2):
        return jnp.where(self.z0, before2, jnp.where(self.z1, before, pltpu.roll(row, 2, 0)))


def ky_up_rows(array):
    return array, swap(array)


def ky_down_rows(array):
    return swap(array), array


def along_kx(sh, u, digit):
    low, centre, high, far = terms(digit, u - sh.kx(u, -1))
    return sh.kx(low, -1) + centre + sh.kx(high + sh.kx(far, 1), 1)


def along_kz(sh, u, digit, above, t_above, digit_b, below, s_below):
    low, centre, high, far = terms(digit, u - sh.kz_next(u, above))
    edge = below - u[0:1]
    far = sh.kz_prev(far, c_far(digit_b) * edge)
    return sh.kz_next(low, t_above) + centre + sh.kz_prev(high + far, c_high(digit_b) * edge + s_below)


def along_ky(sh, rows, digit_rows, above, t_above, digit_b, below, s_below):
    nxt = rows[1:] + [jnp.where(sh.low, swap(rows[0]), above)]
    parts = [terms(digit_rows[r], rows[r] - nxt[r]) for r in range(R)]
    edge = below - rows[0]
    low_after = jnp.where(sh.low, swap(parts[0][0]), t_above)
    high_before = jnp.where(sh.low, c_high(digit_b) * edge, swap(parts[R - 1][2]))
    far_before = jnp.where(sh.low, c_far(digit_b) * edge, swap(parts[R - 1][3]))
    far_before2 = jnp.where(sh.low, s_below, swap(parts[R - 2][3]))
    lows = [p[0] for p in parts] + [low_after]
    highs = [high_before] + [p[2] for p in parts]
    fars = [far_before2, far_before] + [p[3] for p in parts]
    return [lows[r + 1] + parts[r][1] + highs[r] + fars[r] for r in range(R)]


def gather(table, index):
    wide = jnp.broadcast_to(table, (Z, L))
    return jnp.take_along_axis(wide, index, axis=1)


def pos_terms(rows, digit_rows):
    nxt = rows[1:] + [None]
    parts = [
        terms(digit_rows[x], rows[x] - nxt[x] if nxt[x] is not None else rows[x])
        for x in range(X)
    ]
    out = []
    for x in range(X):
        value = parts[x][1]
        if x + 1 < X:
            value = value + parts[x + 1][0]
        if x >= 1:
            value = value + parts[x - 1][2]
        if x >= 2:
            value = value + parts[x - 2][3]
        out.append(value)
    return out


def pos_corrections(first, digit_last, digit_b, below, s_below, above, t_above):
    edge = below - first
    low, centre, _, _ = coeffs(digit_last)
    return (
        c_high(digit_b) * edge + s_below,
        c_far(digit_b) * edge,
        -low * above,
        t_above - centre * above,
    )


def shell_sums(w_ref, shell_ref):
    shells = lax.broadcasted_iota(jnp.int32, (SHELLS, L), 0)

    def body(r, total):
        left = jnp.concatenate(
            [w_ref[r, pl.ds(z, 2 * X, stride=Z), :] for z in range(Z)], axis=1
        ).astype(BF16)
        right = jnp.concatenate(
            [
                jnp.where(shells == shell_ref[r, z : z + 1, :], 1.0, 0.0).astype(BF16)
                for z in range(Z)
            ],
            axis=1,
        )
        return total + lax.dot_general(
            left, right, (((1,), (1,)), ((), ())), preferred_element_type=F32
        )

    both = jnp.zeros((2 * X, SHELLS), F32)
    for r in range(R):
        both = body(r, both)
    return both[:X] + both[X:]


def put_weighted(w_ref, r, x, value):
    head = value.astype(BF16).astype(F32)
    w_ref[r, x * Z : (x + 1) * Z, :] = head
    w_ref[r, (X + x) * Z : (X + x + 1) * Z, :] = value - head


def edges_kernel(
    u_hbm, code_hbm, start_hbm, vel_hbm, field_hbm, pos_up, pos_down, ky_up, ky_down, kz_up, kz_down,
    u_ref, code_ref, start_ref, vel_ref, field_ref, arrived,
):
    pairs = ((u_hbm, u_ref), (code_hbm, code_ref), (vel_hbm, vel_ref), (start_hbm, start_ref), (field_hbm, field_ref))
    copies = [pltpu.make_async_copy(a, b, arrived.at[n]) for n, (a, b) in enumerate(pairs)]
    for copy in copies:
        copy.start()
    for copy in copies[:3]:
        copy.wait()

    def whole(ref, x, r):
        return pack(ref[x, r], ref[x, r + R])

    def plane(ref, x, z):
        both = ref[x, :, z, :]
        return pack(both[:R], both[R:])

    for r in range(R):
        v = pack(vel_ref[r], vel_ref[r + R])
        u0, u1, u2, u3 = (v * whole(u_ref, x, r) for x in range(X))
        d0, d2, d3 = (split6(whole(code_ref, x, r).astype(F32))[1] for x in (0, 2, 3))
        pos_up[0, r] = d3
        pos_up[1, r] = u3
        pos_up[2, r] = c_far(d2) * (u2 - u3)
        pos_down[0, r] = u0
        pos_down[1, r] = c_low(d0) * (u0 - u1)
    copies[3].wait()
    for x in range(X):
        k = 2 * R - 1
        d_last = digits_of(code_ref[x, k].astype(F32))[1]
        d_prev = digits_of(code_ref[x, k - 1].astype(F32))[1]
        last, prev = u_ref[x, k], u_ref[x, k - 1]
        ky_up[0, x] = pack(d_last, last)
        ky_up[1, x] = pack(c_far(d_prev) * (prev - last), start_ref[x, k])
        ky_up[2, x] = pack(start_ref[x, k - 1], start_ref[x, k - 1])
        d_first = digits_of(code_ref[x, 0].astype(F32))[1]
        first, second = u_ref[x, 0], u_ref[x, 1]
        ky_down[0, x] = pack(first, c_low(d_first) * (first - second))
        ky_down[1, x] = pack(start_ref[x, 0], start_ref[x, 1])
        d_last = digits_of(plane(code_ref, x, Z - 1).astype(F32))[2]
        d_prev = digits_of(plane(code_ref, x, Z - 2).astype(F32))[2]
        last, prev = plane(u_ref, x, Z - 1), plane(u_ref, x, Z - 2)
        kz_up[0, x] = d_last
        kz_up[1, x] = last
        kz_up[2, x] = c_far(d_prev) * (prev - last)
        kz_up[3, x] = plane(start_ref, x, Z - 1)
        kz_up[4, x] = plane(start_ref, x, Z - 2)
        d_first = digits_of(plane(code_ref, x, 0).astype(F32))[2]
        first, second = plane(u_ref, x, 0), plane(u_ref, x, 1)
        kz_down[0, x] = first
        kz_down[1, x] = c_low(d_first) * (first - second)
        kz_down[2, x] = plane(start_ref, x, 0)
        kz_down[3, x] = plane(start_ref, x, 1)
    copies[4].wait()


def first_sums_kernel(
    field, u_ref, code_ref, vel_ref, shell_ref, out_ref, in_ref, section_ref, start_ref,
    u_p, code_p, fields_p, shell_p, field_p, section_p, start_p, sums, w_ref,
):
    for c in range(3):
        for x in range(X):
            field_p[c, x] = jnp.broadcast_to(field[c : c + 1, x : x + 1], (R, L))
    for r in range(R):
        fields_p[0, r] = pack(vel_ref[r], vel_ref[r + R])
        weight = pack(out_ref[r], out_ref[r + R])
        fields_p[1, r] = weight
        fields_p[2, r] = pack(in_ref[r], in_ref[r + R])
        shell_p[r] = pack(shell_ref[r], shell_ref[r + R])
        for x in range(X):
            u = pack(u_ref[x, r], u_ref[x, r + R])
            u_p[x, r] = u
            code_p[x, r] = pack(code_ref[x, r], code_ref[x, r + R]).astype(F32)
            section_p[x, r] = pack(section_ref[x, r], section_ref[x, r + R])
            start_p[x, r] = pack(start_ref[x, r], start_ref[x, r + R])
            put_weighted(w_ref, r, x, weight * u)
    totals = shell_sums(w_ref, shell_p)
    tile = jnp.concatenate([totals, jnp.zeros_like(totals)], axis=1)
    for n in range(sums.shape[0]):
        sums[n] = tile


def add_copies(got):
    total = got[0]
    for n in range(1, got.shape[0]):
        total = total + got[n]
    return total


def near_terms(sh, field, x, u, digit, kz_rows):
    ks = (along_kx(sh, u, digit[3]), along_kz(sh, u, digit[2], *kz_rows))
    return ks, field[0, x, 0:1, :] * ks[0] + field[2, x, 0:1, :] * ks[1]


def ky_digit(code):
    return split6(split6(code)[0])[1]


def face(digit, f_prev, f, f_next, f_next2):
    low, centre, high, far = coeffs(digit)
    return low * f_prev + centre * f + high * f_next + far * f_next2


def section_kernel(field, u_p, code_p, fields_p, section_p, start_p, kz_up, kz_down, partial, slopes):
    sh = Shifts()

    def body(x, carry):
        grad_kx, grad_kz = jnp.zeros((Z, L), F32), jnp.zeros((Z, L), F32)
        for r in range(R):
            u, f, d = u_p[x, r], start_p[x, r], digits_of(code_p[x, r])
            up = [kz_up[n, x, r : r + 1, :] for n in range(5)]
            down = [kz_down[n, x, r : r + 1, :] for n in range(4)]
            ks, push = near_terms(sh, field, x, u, d, (down[0], down[1], up[0], up[1], up[2]))
            grad_kx = grad_kx + section_p[x, r] * ks[0]
            grad_kz = grad_kz + section_p[x, r] * ks[1]
            partial[x, r] = push
            faces_kx = face(d[3], sh.kx(f, 1), f, sh.kx(f, -1), sh.kx(f, -2))
            slopes[0, x, r] = faces_kx - sh.kx(faces_kx, 1)
            faces_kz = face(
                d[2], sh.kz_prev(f, up[3]), f, sh.kz_next(f, down[2]), sh.kz_next2(f, down[2], down[3])
            )
            slopes[1, x, r] = faces_kz - sh.kz_prev(faces_kz, face(up[0], up[4], up[3], f[0:1], f[1:2]))
        slopes[0, x, R] = grad_kx
        slopes[1, x, R] = grad_kz
        return carry

    lax.fori_loop(0, X, body, 0)

    def finish(r, carry):
        v = fields_p[0, r]
        us = [u_p[x, r] for x in range(X)]
        k_pos = pos_terms([v * u for u in us], [split6(code_p[x, r])[1] for x in range(X)])
        for x in range(X):
            partial[x, r] = 0.5 * us[x] - (0.5 * time_step) * (partial[x, r] + k_pos[x] + us[x])
        return carry

    lax.fori_loop(0, R, finish, 0)


def section_ky_kernel(given, field, u_p, code_p, section_p, start_p, ky_up, ky_down, partial, slope):
    sh = Shifts()

    def body(x, carry):
        rows = [u_p[x, r] for r in range(R)]
        digit = [ky_digit(code_p[x, r]) for r in range(R)]
        start = [start_p[x, r] for r in range(R)]
        d_b, below = ky_up_rows(ky_up[0, x])
        s_below, f_below = ky_up_rows(ky_up[1, x])
        f_below2 = ky_up[2, x]
        above, t_above = ky_down_rows(ky_down[0, x])
        f_above, f_above2 = ky_down_rows(ky_down[1, x])
        k_ky = along_ky(sh, rows, digit, above, t_above, d_b, below, s_below)
        before = [jnp.where(sh.low, f_below, swap(start[R - 1]))] + start[:-1]
        after = start + [
            jnp.where(sh.low, swap(start[0]), f_above),
            jnp.where(sh.low, swap(start[1]), f_above2),
        ]
        faces = [face(digit[r], before[r], start[r], after[r + 1], after[r + 2]) for r in range(R)]
        face_b = face(d_b, f_below2, f_below, start[0], start[1])
        faces_before = [jnp.where(sh.low, face_b, swap(faces[R - 1]))] + faces[:-1]
        grad = jnp.zeros((Z, L), F32)
        push = (0.5 * time_step) * field[1, x, 0:1, :]
        for r in range(R):
            grad = grad + section_p[x, r] * k_ky[r]
            partial[x, r] = given[x, r] - push * k_ky[r]
            slope[x, r] = faces[r] - faces_before[r]
        slope[x, R] = grad
        return carry

    lax.fori_loop(0, X, body, 0)


def section_edges_kernel(
    partial, u_p, code_p, fields_p, shell_p, got_up, got_down, got_sums, section, pos_up, pos_down
):
    totals = add_copies(got_sums)

    def body(r, carry):
        v, back, shell = fields_p[0, r], fields_p[2, r], shell_p[r]
        d0, d2, d3 = (split6(code_p[x, r])[1] for x in (0, 2, 3))
        more = pos_corrections(
            v * u_p[0, r], d3, got_up[0, r], got_up[1, r], got_up[2, r], got_down[0, r], got_down[1, r]
        )
        m = []
        for x in range(X):
            value = partial[x, r] + (0.5 * time_step) * (back * gather(totals[x : x + 1], shell) - more[x])
            section[x, r] = value
            m.append(v * value)
        pos_up[0, r] = m[3]
        pos_up[1, r] = c_far(d2) * (m[2] - m[3])
        pos_down[0, r] = m[0]
        pos_down[1, r] = c_low(d0) * (m[0] - m[1])
        return carry

    lax.fori_loop(0, R, body, 0)


def momentum_edges_kernel(section, code_p, ky_up, ky_down, kz_up, kz_down):
    low_half = lanes((Z, L)) < HALF
    for x in range(X):
        last, prev = section[x, R - 1], section[x, R - 2]
        far = c_far(digits_of(code_p[x, R - 2])[1]) * (prev - last)
        ky_up[x] = jnp.where(low_half, swap(last), far)
        first, second = section[x, 0], section[x, 1]
        low = c_low(digits_of(code_p[x, 0])[1]) * (first - second)
        ky_down[x] = jnp.where(low_half, first, swap(low))
        last, prev = section[x, :, Z - 1, :], section[x, :, Z - 2, :]
        kz_up[0, x] = last
        kz_up[1, x] = c_far(digits_of(code_p[x, :, Z - 2, :])[2]) * (prev - last)
        first, second = section[x, :, 0, :], section[x, :, 1, :]
        kz_down[0, x] = first
        kz_down[1, x] = c_low(digits_of(code_p[x, :, 0, :])[2]) * (first - second)


def second_sums_kernel(section, fields_p, shell_p, near, slope_ky, sums, w_ref):
    slopes = (near.at[0], slope_ky, near.at[1])
    row = lax.broadcasted_iota(jnp.int32, (X, SHELLS), 0)
    column = lax.broadcasted_iota(jnp.int32, (X, SHELLS), 1)
    inner = jnp.zeros((X, SHELLS), F32)
    for x in range(X):
        parts = [(0.5 * time_step) * slopes[c][x, R] for c in range(3)]
        for r in range(R):
            value = section[x, r]
            put_weighted(w_ref, r, x, fields_p[1, r] * value)
            parts = [p + time_step * (value * slopes[c][x, r]) for c, p in enumerate(parts)]
        for c in range(3):
            whole = jnp.sum(jnp.sum(parts[c], axis=0, keepdims=True), axis=1, keepdims=True)
            inner = inner - jnp.where((row == x) & (column == c), whole, 0.0)
    tile = jnp.concatenate([shell_sums(w_ref, shell_p), inner], axis=1)
    for n in range(sums.shape[0]):
        sums[n] = tile


def interior_kernel(field, section, u_p, code_p, fields_p, first_kz, kz_up, kz_down, partial):
    sh = Shifts()

    def body(x, carry):
        for r in range(R):
            here = slice(r, r + 1)
            kz_rows = (
                kz_down[0, x, here, :],
                kz_down[1, x, here, :],
                first_kz[0, x, here, :],
                kz_up[0, x, here, :],
                kz_up[1, x, here, :],
            )
            _, push = near_terms(sh, field, x, section[x, r], digits_of(code_p[x, r]), kz_rows)
            partial[x, r] = push
        return carry

    lax.fori_loop(0, X, body, 0)

    def finish(r, carry):
        v = fields_p[0, r]
        ms = [section[x, r] for x in range(X)]
        k_pos = pos_terms([v * m for m in ms], [split6(code_p[x, r])[1] for x in range(X)])
        for x in range(X):
            partial[x, r] = (
                0.5 * u_p[x, r] + ms[x] - time_step * (partial[x, r] + k_pos[x] + ms[x])
            )
        return carry

    lax.fori_loop(0, R, finish, 0)


def interior_ky_kernel(given, field, section, code_p, first_up, ky_up, ky_down, partial):
    sh = Shifts()

    def body(x, carry):
        rows = [section[x, r] for r in range(R)]
        digit = [ky_digit(code_p[x, r]) for r in range(R)]
        below, s_below = ky_up_rows(ky_up[x])
        above, t_above = ky_down_rows(ky_down[x])
        k_ky = along_ky(sh, rows, digit, above, t_above, first_up[0, x], below, s_below)
        push = time_step * field[1, x, 0:1, :]
        for r in range(R):
            partial[x, r] = given[x, r] - push * k_ky[r]
        return carry

    lax.fori_loop(0, X, body, 0)


def result_kernel(
    scale, partial, section, code_p, fields_p, shell_p, first_up, got_up, got_down, got_sums, state, grad
):
    totals = add_copies(got_sums)
    for r in range(R):
        v, back, shell = fields_p[0, r], fields_p[2, r], shell_p[r]
        more = pos_corrections(
            v * section[0, r], split6(code_p[3, r])[1], first_up[0, r], got_up[0, r], got_up[1, r],
            got_down[0, r], got_down[1, r],
        )
        for x in range(X):
            value = partial[x, r] + time_step * (back * gather(totals[x : x + 1], shell) - more[x])
            state[x, r] = value[:, :HALF]
            state[x, r + R] = value[:, HALF:]
    row = lax.broadcasted_iota(jnp.int32, (X, L), 0)
    column = lanes((X, L))
    for c in range(3):
        spread = jnp.broadcast_to(totals[:, SHELLS + c : SHELLS + c + 1], (X, L))
        line = jnp.sum(jnp.where(row == column, spread, 0.0), axis=0, keepdims=True)
        grad[c : c + 1, :] = line[:, :X] * scale


def call(kernel, outs, args, in_hbm=False, scratch=(), ops=0, aliases={}):
    if in_hbm:
        args = [pltpu.with_memory_space_constraint(a, pltpu.HBM) for a in args]
    shapes = [jax.ShapeDtypeStruct(shape, F32 if dtype is None else dtype) for shape, dtype in outs]
    moved = sum(4 * a.size for a in args) + sum(4 * s.size for s in shapes)
    vmem = pl.BlockSpec(memory_space=pltpu.VMEM)
    given = pl.BlockSpec(memory_space=pltpu.HBM) if in_hbm else vmem
    return pl.pallas_call(
        kernel,
        out_shape=shapes,
        in_specs=[given] * len(args),
        out_specs=[vmem] * len(shapes),
        scratch_shapes=list(scratch),
        input_output_aliases=aliases,
        compiler_params=pltpu.CompilerParams(vmem_limit_bytes=VMEM_LIMIT),
        cost_estimate=pl.CostEstimate(flops=ops, bytes_accessed=moved, transcendentals=0),
    )(*args)


def shift(array, axis, by, wrap=True):
    count = lax.axis_size(axis)
    pairs = [(i, (i + by) % count) for i in range(count) if wrap or 0 <= i + by < count]
    return lax.ppermute(array, axis, pairs)


def shift_both(up, down, axis, wrap=True):
    up = shift(up, axis, 1, wrap)
    down = shift(down, axis, -1, wrap)
    return up, down


def exchange(copies):
    return lax.all_to_all(copies, ("ky", "kz"), 0, 0)


def shards(
    cotangent,
    start_state,
    section_state,
    face_codes,
    field_strength,
    velocity,
    shell_index,
    shell_out,
    shell_in,
):
    members = lax.axis_size("ky") * lax.axis_size("kz")
    plane, ky_plane, kz_plane = (R, Z, L), (X, Z, L), (X, R, L)
    w_scratch = [pltpu.VMEM((R, 2 * X * Z, L), F32)]
    sums_shape = ((members, X, L), None)
    up, down, ky_up, ky_down, kz_up, kz_down, u_v, code_v, start_v, vel_v, field_v = call(
        edges_kernel,
        [((3,) + plane, None), ((2,) + plane, None), ((3,) + ky_plane, None), ((2,) + ky_plane, None),
         ((5,) + kz_plane, None), ((4,) + kz_plane, None), (cotangent.shape, None), (cotangent.shape, jnp.int32),
         (cotangent.shape, None), (velocity.shape, None), (field_strength.shape, None)],
        [cotangent, face_codes, start_state, velocity, field_strength],
        in_hbm=True,
        scratch=[pltpu.SemaphoreType.DMA((5,))],
        ops=4_000_000,
    )
    up, down = shift_both(up, down, "pos", False)
    ky_up, ky_down = shift_both(ky_up, ky_down, "ky")
    kz_up, kz_down = shift_both(kz_up, kz_down, "kz")
    u_p, code_p, fields_p, shell_p, field_p, section_p, start_p, sums = call(
        first_sums_kernel,
        [(FULL, None), (FULL, None), ((3,) + plane, None), (plane, jnp.int32), ((3, X, R, L), None),
         (FULL, None), (FULL, None), sums_shape],
        [field_v, u_v, code_v, vel_v, shell_index, shell_out, shell_in, section_state, start_v],
        scratch=w_scratch,
        ops=8_000_000,
    )
    sums = exchange(sums)
    partial, near = call(
        section_kernel,
        [(FULL, None), ((2, X, R + 1, Z, L), None)],
        [field_p, u_p, code_p, fields_p, section_p, start_p, kz_up, kz_down],
        ops=12_000_000,
    )
    partial, slope_ky = call(
        section_ky_kernel,
        [(FULL, None), ((X, R + 1, Z, L), None)],
        [partial, field_p, u_p, code_p, section_p, start_p, ky_up, ky_down],
        aliases={0: 0},
        ops=5_000_000,
    )
    section, up2, down2 = call(
        section_edges_kernel,
        [(FULL, None), ((2,) + plane, None), ((2,) + plane, None)],
        [partial, u_p, code_p, fields_p, shell_p, up, down, sums],
        aliases={0: 0},
        ops=2_000_000,
    )
    up2, down2 = shift_both(up2, down2, "pos", False)
    ky_up2, ky_down2, kz_up2, kz_down2 = call(
        momentum_edges_kernel,
        [(ky_plane, None), (ky_plane, None), ((2,) + kz_plane, None), ((2,) + kz_plane, None)],
        [section, code_p],
        ops=1_000_000,
    )
    ky_up2, ky_down2 = shift_both(ky_up2, ky_down2, "ky")
    kz_up2, kz_down2 = shift_both(kz_up2, kz_down2, "kz")
    (sums2,) = call(
        second_sums_kernel, [sums_shape], [section, fields_p, shell_p, near, slope_ky], scratch=w_scratch, ops=4_000_000
    )
    sums2 = exchange(sums2)
    (partial2,) = call(
        interior_kernel,
        [(FULL, None)],
        [field_p, section, u_p, code_p, fields_p, kz_up, kz_up2, kz_down2],
        ops=6_000_000,
    )
    (partial2,) = call(
        interior_ky_kernel,
        [(FULL, None)],
        [partial2, field_p, section, code_p, ky_up, ky_up2, ky_down2],
        aliases={0: 0},
        ops=2_000_000,
    )
    state_adjoint, field_grad = call(
        functools.partial(result_kernel, 1.0 / (KX * KY * KZ) ** 0.5),
        [((X, 2 * R, Z, HALF), None), ((3, X), None)],
        [partial2, section, code_p, fields_p, shell_p, up, up2, down2, sums2],
        ops=3_000_000,
    )
    return (state_adjoint, field_grad)


def solution(mesh):
    return jax.shard_map(
        shards,
        mesh=mesh,
        in_specs=(
            P("pos", "ky", "kz", None),
            P("pos", "ky", "kz", None),
            P("pos", "ky", "kz", None),
            P("pos", "ky", "kz", None),
            P(None, "pos"),
            P("ky", "kz", None),
            P("ky", "kz", None),
            P("ky", "kz", None),
            P("ky", "kz", None),
        ),
        out_specs=(P("pos", "ky", "kz", None), P(None, "pos")),
        check_vma=False,
    )
```
